256 devices in a mesh: row: 32 (over y, z_lo, core), col: 8 (over x, z_hi).
Axes of the slice: x: 4, y: 4, z: 8 (z_hi: 2, z_lo: 4; z = z_hi * 4 + z_lo), core: 2. Of those that a mesh axis runs over, the one named last changes fastest.
Arguments:
- vectors: float32 [32, 524288], P(None, ('row', 'col')), may hold values from -6 to 6
- block_values: bfloat16 [65536, 128, 128], P(('row', 'col')), may hold values from -0.15625 to 0.15625
- block_rows: int32 [65536], P(('row', 'col')), may hold values from 0 to 127, as said below
- block_cols: int32 [65536], P(('row', 'col')), may hold values from 0 to 511, as said below
- block_counts: int32 [256], P(('row', 'col')), may hold values from 32 to 256, as said below
- center: float32 [1], replicated, may hold values from -0.5 to 0.5
- radius: float32 [1], replicated, may hold values from 1.5 to 3
Outputs:
- filtered: float32 [32, 524288], P(None, ('row', 'col'))
The draws below stay inside these ranges and needn't reach their ends.
Inputs may be any that keep to these rules, and one draw needn't show every extreme that they name: `block_counts`: live slots of each device; some device fills all 256 slots. `block_rows`: Block-row inside the row group; slots may repeat a position. `block_cols`: Block-column inside the col group; slots may repeat a position.
All inputs are finite; a program needn't handle non-finite values.
Results may differ from the reference program's by a relative error of at most 0.02.
Values may be sent and summed in bfloat16 or wider, within the bound.
A program may use at most 128 MiB of HBM per device.

```python
import jax
import jax.numpy as jnp
from jax import lax

K = 32
BS = 128
ROWS_DEV = 2048
CAP = 256
STEPS = 2
N = 524288
BLK_ROWS = 128
BLK_COLS = 512
SLOTS = 65536
N_ROW = 32
N_COL = 8


def draw_block_counts(key, part):
    device_total = SLOTS // CAP
    drawn_values = jax.random.randint(jax.random.fold_in(key, 11), (device_total,), 0, CAP + 1)
    counts_all = jnp.maximum(max(CAP // 8, 1), drawn_values * drawn_values // CAP)
    busiest = jax.random.randint(jax.random.fold_in(key, 12), (), 0, device_total)
    counts_all = counts_all.at[busiest].set(CAP)
    counts_all = counts_all.at[(busiest + 1) % device_total].set(max(CAP // 8, 1))
    return counts_all.astype(jnp.int32)


def draw_block_rows(key, part):
    picked = jax.random.randint(jax.random.fold_in(key, 21), (SLOTS,), 0, BLK_ROWS)
    picked = picked.at[0].set(0).at[1].set(BLK_ROWS - 1)
    return picked.astype(jnp.int32)


def draw_block_cols(key, part):
    picked = jax.random.randint(jax.random.fold_in(key, 31), (SLOTS,), 0, BLK_COLS)
    picked = picked.at[0].set(0).at[1].set(BLK_COLS - 1)
    return picked.astype(jnp.int32)


def block_scale(key, dims, split, least, largest):
    factor_of = 1.0
    for dim, blocks in split:
        draws = jax.random.uniform(jax.random.fold_in(jax.random.fold_in(key, 6), dim), (blocks,), jnp.float32, least / len(split), largest / len(split))
        factor_of = factor_of * jnp.repeat(jnp.exp(draws), dims[dim] // blocks).reshape((-1,) + (1,) * (len(dims) - 1 - dim))
    return factor_of


def normal_values(stream_key, dims, width, bound, cuts=(), held_as=jnp.bfloat16):
    level = block_scale(stream_key, dims, cuts, -0.22, 0.18) if cuts else 1.0
    result = jax.random.normal(stream_key, dims, jnp.float32) * width * level
    return jnp.minimum(jnp.maximum(result, -bound), bound).astype(held_as)


def setup_inputs(seed: int = 0) -> dict:
    keys = jax.random.split(jax.random.key(seed), 8)
    return {
        "vectors": normal_values(keys[0], (K, N), 1.0, 6.0, ((1, 256),), jnp.float32),
        "block_values": normal_values(keys[1], (SLOTS, BS, BS), (2 * CAP * BS * BS // (3 * ROWS_DEV)) ** -0.5, 0.15625, ((0, 256),)),
        "block_rows": draw_block_rows(jax.random.fold_in(keys[7], 71), 0),
        "block_cols": draw_block_cols(jax.random.fold_in(keys[7], 71), 0),
        "block_counts": draw_block_counts(jax.random.fold_in(keys[7], 71), 0),
        "center": jnp.clip(jax.random.uniform(keys[5], (1,), jnp.float32, -0.5, 0.5), -0.5, 0.5),
        "radius": jnp.clip(jax.random.uniform(keys[6], (1,), jnp.float32, 1.5, 3.0), 1.5, 3.0),
    }


def rounded(values):
    return lax.optimization_barrier(values.astype(jnp.bfloat16)).astype(jnp.float32)


def reference(vectors, block_values, block_rows, block_cols, block_counts, center, radius):
    center_value = center[0]
    radius_value = radius[0]

    def apply_operator(current):
        narrow = current.astype(jnp.bfloat16).reshape(K, N_ROW, N_COL, ROWS_DEV)

        def device_term(device_index, image_sum):
            row_index = device_index // N_COL
            col_index = device_index % N_COL
            row_region = lax.dynamic_index_in_dim(narrow, row_index, 1, keepdims=False).reshape(K, BLK_ROWS, BS).astype(jnp.float32)
            col_region = lax.dynamic_index_in_dim(narrow, col_index, 2, keepdims=False).reshape(K, BLK_COLS, BS).astype(jnp.float32)
            first_slot = (device_index * CAP).astype(jnp.int32)
            blocks = lax.dynamic_slice_in_dim(block_values, first_slot, CAP, 0).astype(jnp.float32)
            rows_here = lax.dynamic_slice_in_dim(block_rows, first_slot, CAP, 0).astype(jnp.int32)
            cols_here = lax.dynamic_slice_in_dim(block_cols, first_slot, CAP, 0).astype(jnp.int32)
            live_slots = (jnp.arange(CAP, dtype=jnp.int32) < block_counts[device_index]).astype(jnp.float32)[:, None, None]
            forward = jnp.einsum("sij,ksj->ski", blocks, jnp.take(col_region, cols_here, axis=1)) * live_slots
            forward = jax.ops.segment_sum(forward, rows_here, num_segments=BLK_ROWS)
            mirror = jnp.einsum("sij,ksi->skj", blocks, jnp.take(row_region, rows_here, axis=1)) * live_slots
            mirror = jax.ops.segment_sum(mirror, cols_here, num_segments=BLK_COLS)
            forward = rounded(jnp.transpose(forward, (1, 0, 2)).reshape(K, N_COL, ROWS_DEV))
            mirror = rounded(jnp.transpose(mirror, (1, 0, 2)).reshape(K, N_ROW, ROWS_DEV))
            image_sum = image_sum.at[:, row_index].add(forward)
            image_sum = image_sum.at[:, :, col_index].add(mirror)
            return image_sum

        start_image = jnp.zeros((K, N_ROW, N_COL, ROWS_DEV), jnp.float32)
        image_sum = lax.fori_loop(0, N_ROW * N_COL, device_term, start_image)
        return image_sum.reshape(K, N)

    previous = vectors
    current = (apply_operator(vectors) - center_value * vectors) / radius_value
    for repeat_index in range(STEPS - 1):
        following = 2.0 * (apply_operator(current) - center_value * current) / radius_value - previous
        previous = current
        current = following
    return current
```

```python
import functools

import jax
import jax.numpy as jnp
from jax import lax
from jax.experimental import pallas as pl
from jax.experimental.pallas import tpu as pltpu
from jax.sharding import PartitionSpec as P

MESH = pl.DeviceIdType.MESH
BF16, F32 = jnp.bfloat16, jnp.float32
ANY = pl.BlockSpec(memory_space=pl.ANY)
VMEM = pl.BlockSpec(memory_space=pltpu.VMEM)
SMEM = pl.BlockSpec(memory_space=pltpu.SMEM)


class Place:
    def __init__(self):
        row, col = lax.axis_index("row"), lax.axis_index("col")
        self.row, self.col = row, col
        self.y, self.z, self.c = row // 8, (row // 2) % 4, row % 2
        self.x, self.h = col // 2, col % 2

    def row_of(self, y=None, z=None, c=None):
        y = self.y if y is None else y
        z = self.z if z is None else z
        c = self.c if c is None else c
        return (y * 4 + z) * 2 + c

    def at_y(self, step):
        return (self.row_of(y=(self.y + step) % 4), self.col)

    def at_z(self, z):
        return (self.row_of(z=z), self.col)

    def at_x(self, step):
        return (self.row, ((self.x + step) % 4) * 2 + self.h)

    def other_core(self):
        return (self.row_of(c=1 - self.c), self.col)

    def ring_z(self, step):
        zz = (self.h * 4 + self.z + 8 + step) % 8
        return (self.row_of(z=zz % 4), self.x * 2 + zz // 4)

    def half_of(self, step):
        return ((self.h * 4 + self.z + 8 + step) % 8) // 4

    def z_order(self):
        z = self.z
        return [z + 1 - 2 * (z % 2), (z + 2) % 4, 3 - z]

    def partners(self):
        found = [self.at_z(z) for z in self.z_order()]
        found += [self.at_y(1), self.at_y(3), self.at_x(1), self.at_x(3), self.other_core()]
        return found + [self.ring_z(2), self.ring_z(-2)]


class Wire:
    def __init__(self, send_sems, recv_sems):
        self.send_sems, self.recv_sems, self.copies = send_sems, recv_sems, []

    def send(self, src, dst, device):
        index = len(self.copies)
        copy = pltpu.make_async_remote_copy(
            src_ref=src,
            dst_ref=dst,
            send_sem=self.send_sems.at[index],
            recv_sem=self.recv_sems.at[index],
            device_id=device,
            device_id_type=MESH,
        )
        copy.start()
        self.copies.append(copy)
        return copy

    def drain(self):
        for copy in self.copies:
            copy.wait_send()


def greet(place):
    barrier = pltpu.get_barrier_semaphore()
    partners = place.partners()
    for partner in partners:
        pl.semaphore_signal(barrier, inc=1, device_id=partner, device_id_type=MESH)
    return barrier, len(partners)


def add_blocks(target, addend, count):
    def body(b, carry):
        target[b] = target[b] + addend[b]
        return carry

    lax.fori_loop(0, count, body, 0)


def gather_parts(place, wire, own, cols_out, rows_out, relay, local_sems):
    nb = own.shape[0]
    hf = nb // 2
    y, z, c, x, h = place.y, place.z, place.c, place.x, place.h

    def cc(yy, zz):
        return cols_out.at[pl.ds(place.row_of(y=yy, z=zz) * nb, nb)]

    def cc_half(yy, zz, part):
        return cols_out.at[pl.ds(place.row_of(y=yy, z=zz) * nb + part * hf, hf)]

    def rr(xx, hh):
        return rows_out.at[pl.ds((xx * 2 + hh) * nb, nb)]

    def rr_half(xx, hh, part):
        return rows_out.at[pl.ds((xx * 2 + hh) * nb + part * hf, hf)]

    mine_cc, mine_rr = cc(y, z), rr(x, h)
    zs = place.z_order()
    z_copies = [wire.send(own, mine_cc, place.at_z(zz)) for zz in zs]
    relay_a = wire.send(own.at[pl.ds(0, hf)], relay.at[pl.ds(0, hf)], place.ring_z(2))
    relay_b = wire.send(own.at[pl.ds(hf, hf)], relay.at[pl.ds(hf, hf)], place.ring_z(-2))
    ups = [wire.send(own, mine_cc, place.at_y(1))]
    downs = [wire.send(own, mine_cc, place.at_y(3))]
    rights = [wire.send(own, mine_rr, place.at_x(1))]
    lefts = [wire.send(own, mine_rr, place.at_x(3))]
    cores = [wire.send(own, mine_cc, place.other_core())]
    keep_cc = pltpu.make_async_copy(own, mine_cc, local_sems.at[0])
    keep_rr = pltpu.make_async_copy(own, mine_rr, local_sems.at[1])
    keep_cc.start()
    keep_rr.start()
    order = [z] + zs
    up_halves, down_halves, right_halves, left_halves = [], [], [], []

    def forward_y(k):
        ups[k].wait_recv()
        up_halves.append(wire.send(cc_half((y + 3) % 4, order[k], 0), cc_half((y + 3) % 4, order[k], 0), place.at_y(1)))
        cores.append(wire.send(cc((y + 3) % 4, order[k]), cc((y + 3) % 4, order[k]), place.other_core()))
        downs[k].wait_recv()
        down_halves.append(wire.send(cc_half((y + 1) % 4, order[k], 1), cc_half((y + 1) % 4, order[k], 1), place.at_y(3)))
        cores.append(wire.send(cc((y + 1) % 4, order[k]), cc((y + 1) % 4, order[k]), place.other_core()))

    def forward_x(k, hh):
        rights[k].wait_recv()
        right_halves.append(wire.send(rr_half((x + 3) % 4, hh, 0), rr_half((x + 3) % 4, hh, 0), place.at_x(1)))
        lefts[k].wait_recv()
        left_halves.append(wire.send(rr_half((x + 1) % 4, hh, 1), rr_half((x + 1) % 4, hh, 1), place.at_x(3)))

    def pass_on_z(k):
        z_copies[k].wait_recv()
        piece = cc(y, zs[k])
        ups.append(wire.send(piece, piece, place.at_y(1)))
        downs.append(wire.send(piece, piece, place.at_y(3)))
        cores.append(wire.send(piece, piece, place.other_core()))

    relay_a.wait_recv()
    far_a = wire.send(relay.at[pl.ds(0, hf)], rr_half(x, place.half_of(-2), 0), place.ring_z(2))
    relay_b.wait_recv()
    far_b = wire.send(relay.at[pl.ds(hf, hf)], rr_half(x, place.half_of(2), 1), place.ring_z(-2))
    pass_on_z(0)
    forward_y(0)
    forward_x(0, h)
    pass_on_z(1)
    far_a.wait_recv()
    far_b.wait_recv()
    far = rr(x, 1 - h)
    rights.append(wire.send(far, far, place.at_x(1)))
    lefts.append(wire.send(far, far, place.at_x(3)))
    forward_y(1)
    pass_on_z(2)
    forward_x(1, 1 - h)
    forward_y(2)
    forward_y(3)
    for k in range(4):
        up_halves[k].wait_recv()
        down_halves[k].wait_recv()
        piece = cc((y + 2) % 4, order[k])
        cores.append(wire.send(piece, piece, place.other_core()))
    for copy in right_halves + left_halves + cores:
        copy.wait_recv()
    keep_cc.wait()
    keep_rr.wait()


def scatter_parts(place, wire, mirror, forward, s, ca, near, d, sf, near_f, relay, v, local_sems):
    nb = v.shape[0]
    hf = nb // 2
    y, z, c, x, h = place.y, place.z, place.c, place.x, place.h
    zs = place.z_order()
    order = [zs[2], zs[1], zs[0], z]
    halves = [1 - h, h]
    bp, bm, cp, cm = near
    ep, em, gp, gm = near_f
    core_copies, locals_m, locals_f = [], [], []
    for k in range(4):
        core_copies.append(wire.send(mirror.at[:, order[k], 1 - c], ca.at[k], place.other_core()))
        local = pltpu.make_async_copy(mirror.at[:, order[k], c], s.at[k], local_sems.at[k])
        local.start()
        locals_m.append(local)
    for k in range(2):
        local = pltpu.make_async_copy(forward.at[:, halves[k]], sf.at[k], local_sems.at[4 + k])
        local.start()
        locals_f.append(local)
    first, last = pl.ds(0, hf), pl.ds(hf, hf)
    x_first = []
    for k in range(2):
        locals_f[k].wait()
        across = sf.at[k, (x + 2) % 4]
        x_first.append((
            wire.send(across.at[first], ep.at[k], place.at_x(1)),
            wire.send(across.at[last], em.at[k], place.at_x(3)),
        ))
    y_first = []
    for k in range(4):
        locals_m[k].wait()
        core_copies[k].wait_recv()
        across = (y + 2) % 4
        add_blocks(s.at[k, across], ca.at[k, across], nb)
        y_first.append((
            wire.send(s.at[k, across, first], bp.at[k], place.at_y(1)),
            wire.send(s.at[k, across, last], bm.at[k], place.at_y(3)),
        ))
        for step in (1, 3):
            add_blocks(s.at[k, (y + step) % 4], ca.at[k, (y + step) % 4], nb)
    x_second, y_second = [], []

    def second_x(k):
        x_first[k][0].wait_recv()
        add_blocks(sf.at[k, (x + 1) % 4, first], ep.at[k], hf)
        x_first[k][1].wait_recv()
        add_blocks(sf.at[k, (x + 3) % 4, last], em.at[k], hf)
        x_second.append((
            wire.send(sf.at[k, (x + 1) % 4], gp.at[k], place.at_x(1)),
            wire.send(sf.at[k, (x + 3) % 4], gm.at[k], place.at_x(3)),
        ))

    def second_y(k):
        y_first[k][0].wait_recv()
        add_blocks(s.at[k, (y + 1) % 4, first], bp.at[k], hf)
        up = wire.send(s.at[k, (y + 1) % 4], cp.at[k], place.at_y(1))
        y_first[k][1].wait_recv()
        add_blocks(s.at[k, (y + 3) % 4, last], bm.at[k], hf)
        y_second.append((up, wire.send(s.at[k, (y + 3) % 4], cm.at[k], place.at_y(3))))

    second_x(0)
    second_y(0)
    second_x(1)
    second_y(1)
    second_y(2)
    second_y(3)
    x_second[0][0].wait_recv()
    x_second[0][1].wait_recv()
    far = sf.at[0, x]

    def sum_far(b, carry):
        total = far[b].astype(F32) + gp[0, b].astype(F32) + gm[0, b].astype(F32)
        far[b] = total.astype(BF16)
        return carry

    lax.fori_loop(0, nb, sum_far, 0)
    relay_a = wire.send(far.at[first], relay.at[first], place.ring_z(2))
    relay_b = wire.send(far.at[last], relay.at[last], place.ring_z(-2))
    z_copies = []

    def third(k):
        y_second[k][0].wait_recv()
        y_second[k][1].wait_recv()
        home = s.at[k, y]

        def sum_home(b, carry):
            total = home[b].astype(F32) + ca[k, y, b].astype(F32)
            total = total + cp[k, b].astype(F32) + cm[k, b].astype(F32)
            home[b] = total.astype(BF16)
            return carry

        lax.fori_loop(0, nb, sum_home, 0)
        z_copies.append(wire.send(home, d.at[k], place.at_z(order[k])))

    third(0)
    relay_a.wait_recv()
    far_a = wire.send(relay.at[first], v.at[first], place.ring_z(2))
    relay_b.wait_recv()
    far_b = wire.send(relay.at[last], v.at[last], place.ring_z(-2))
    third(1)
    third(2)
    for copy in x_second[1] + y_second[3]:
        copy.wait_recv()
    for copy in z_copies + [far_a, far_b]:
        copy.wait_recv()

    def image(b):
        total = s[3, y, b].astype(F32) + ca[3, y, b].astype(F32)
        total = total + cp[3, b].astype(F32) + cm[3, b].astype(F32)
        total = total + d[0, b].astype(F32) + d[1, b].astype(F32) + d[2, b].astype(F32)
        total = total + sf[1, x, b].astype(F32) + gp[1, b].astype(F32) + gm[1, b].astype(F32)
        return total + v[b].astype(F32)

    return image


def gather_kernel(vectors, cols_out, rows_out, own, relay, send_sems, recv_sems, local_sems):
    place = Place()
    barrier, expected = greet(place)
    bs = own.shape[2]
    for b in range(own.shape[0]):
        own[b] = vectors[:, b * bs : (b + 1) * bs].astype(BF16)
    pl.semaphore_wait(barrier, expected)
    wire = Wire(send_sems, recv_sems)
    gather_parts(place, wire, own, cols_out, rows_out, relay, local_sems)
    wire.drain()


SCATTER_SCRATCH = 16


def scatter_scratch(nb, k, bs):
    block = (nb, k, bs)
    half = (nb // 2, k, bs)
    return [
        pltpu.VMEM((4, 4) + block, BF16),
        pltpu.VMEM((4, 4) + block, BF16),
        pltpu.VMEM((4,) + half, BF16),
        pltpu.VMEM((4,) + half, BF16),
        pltpu.VMEM((4,) + block, BF16),
        pltpu.VMEM((4,) + block, BF16),
        pltpu.VMEM((3,) + block, BF16),
        pltpu.VMEM((2, 4) + block, BF16),
        pltpu.VMEM((2,) + half, BF16),
        pltpu.VMEM((2,) + half, BF16),
        pltpu.VMEM((2,) + block, BF16),
        pltpu.VMEM((2,) + block, BF16),
        pltpu.VMEM(block, BF16),
        pltpu.VMEM(block, BF16),
        pltpu.SemaphoreType.DMA((40,)),
        pltpu.SemaphoreType.DMA((40,)),
        pltpu.SemaphoreType.DMA((6,)),
    ]


def run_scatter(place, wire, mirror, forward, scratch):
    s, ca, bp, bm, cp, cm, d, sf, ep, em, gp, gm, relay, v = scratch[:14]
    return scatter_parts(
        place, wire, mirror, forward, s, ca, (bp, bm, cp, cm), d, sf, (ep, em, gp, gm), relay, v, scratch[16]
    )


def middle_kernel(
    mirror, forward, previous, center, radius, cols_out, rows_out, current, *scratch
):
    place = Place()
    barrier, expected = greet(place)
    scatter, (own, relay, send_sems, recv_sems, local_sems) = scratch[:17], scratch[17:]
    pl.semaphore_wait(barrier, expected)
    wire = Wire(scatter[14], scatter[15])
    image = run_scatter(place, wire, mirror, forward, scatter)
    bs = own.shape[2]
    for b in range(own.shape[0]):
        part = slice(b * bs, (b + 1) * bs)
        value = (image(b) - center[0] * previous[:, part]) / radius[0]
        current[:, part] = value
        own[b] = value.astype(BF16)
    second = Wire(send_sems, recv_sems)
    gather_parts(place, second, own, cols_out, rows_out, relay, local_sems)
    wire.drain()
    second.drain()


def last_kernel(mirror, forward, previous, before, center, radius, result, *scratch):
    place = Place()
    barrier, expected = greet(place)
    pl.semaphore_wait(barrier, expected)
    wire = Wire(scratch[14], scratch[15])
    image = run_scatter(place, wire, mirror, forward, scratch)
    nb, bs = scratch[13].shape[0], scratch[13].shape[2]
    for b in range(nb):
        part = slice(b * bs, (b + 1) * bs)
        value = 2.0 * (image(b) - center[0] * previous[:, part]) / radius[0] - before[:, part]
        result[:, part] = value
    wire.drain()


def product_kernel(
    chunk, rows, cols, counts, blocks, col_source, row_source, mirror, forward, mirror_sum, forward_sum
):
    step = pl.program_id(0)
    count = counts[0]
    row_total, col_total = row_source.shape[0], col_source.shape[0]

    @pl.when(step == 0)
    def _():
        mirror_sum[...] = jnp.zeros_like(mirror_sum)
        forward_sum[...] = jnp.zeros_like(forward_sum)

    @pl.when(step * chunk < count)
    def _():
        terms = []
        for i in range(chunk):
            slot = step * chunk + i
            row, col = rows[slot], cols[slot]
            block = blocks[i]
            forward_term = lax.dot_general(
                col_source[col], block, (((1,), (1,)), ((), ())), preferred_element_type=F32
            )
            mirror_term = lax.dot_general(
                row_source[row], block, (((1,), (0,)), ((), ())), preferred_element_type=F32
            )
            live = slot < count
            terms.append((
                jnp.where(live, row, row_total), jnp.where(live, col, col_total), forward_term, mirror_term
            ))
        for row, col, forward_term, mirror_term in terms:
            forward_sum[row] += forward_term
            mirror_sum[col] += mirror_term

    @pl.when(step == pl.num_programs(0) - 1)
    def _():
        def narrow_mirror(b, carry):
            mirror[b] = mirror_sum[b].astype(BF16)
            return carry

        def narrow_forward(b, carry):
            forward[b] = forward_sum[b].astype(BF16)
            return carry

        lax.fori_loop(0, col_total, narrow_mirror, 0, unroll=8)
        lax.fori_loop(0, row_total, narrow_forward, 0, unroll=8)


CHUNK = 16


def products(block_values, rows, cols, counts, col_source, row_source):
    capacity, bs, _ = block_values.shape
    col_total, k, _ = col_source.shape
    row_total = row_source.shape[0]
    whole = lambda i, r, c, n: (0, 0, 0)
    once = pl.Buffered(1)
    return pl.pallas_call(
        functools.partial(product_kernel, CHUNK),
        out_shape=(
            jax.ShapeDtypeStruct((col_total, k, bs), BF16),
            jax.ShapeDtypeStruct((row_total, k, bs), BF16),
        ),
        grid_spec=pltpu.PrefetchScalarGridSpec(
            num_scalar_prefetch=3,
            grid=(capacity // CHUNK,),
            in_specs=[
                pl.BlockSpec((CHUNK, bs, bs), lambda i, r, c, n: (jnp.minimum(i, (n[0] - 1) // CHUNK), 0, 0)),
                pl.BlockSpec((col_total, k, bs), whole, pipeline_mode=once),
                pl.BlockSpec((row_total, k, bs), whole, pipeline_mode=once),
            ],
            out_specs=[
                pl.BlockSpec((col_total, k, bs), whole, pipeline_mode=once),
                pl.BlockSpec((row_total, k, bs), whole, pipeline_mode=once),
            ],
            scratch_shapes=[
                pltpu.VMEM((col_total + 1, k, bs), F32),
                pltpu.VMEM((row_total + 1, k, bs), F32),
            ],
        ),
        compiler_params=pltpu.CompilerParams(
            dimension_semantics=("arbitrary",), vmem_limit_bytes=40 * 2**20
        ),
    )(rows, cols, counts, block_values, col_source, row_source)


def shards(vectors, block_values, block_rows, block_cols, block_counts, center, radius):
    k, own_rows = vectors.shape
    bs = block_values.shape[1]
    nb = own_rows // bs
    row_total = lax.axis_size("col") * nb
    col_total = lax.axis_size("row") * nb
    gathered = (
        jax.ShapeDtypeStruct((col_total, k, bs), BF16),
        jax.ShapeDtypeStruct((row_total, k, bs), BF16),
    )
    whole_vectors = jax.ShapeDtypeStruct((k, own_rows), F32)
    gather_scratch = [
        pltpu.VMEM((nb, k, bs), BF16),
        pltpu.VMEM((nb, k, bs), BF16),
        pltpu.SemaphoreType.DMA((56,)),
        pltpu.SemaphoreType.DMA((56,)),
        pltpu.SemaphoreType.DMA((2,)),
    ]

    def params(index):
        return pltpu.CompilerParams(
            collective_id=index, has_side_effects=True, vmem_limit_bytes=32 * 2**20
        )

    def apart(partials):
        mirror, forward = partials
        return mirror.reshape(4, 4, 2, nb, k, bs), forward.reshape(4, 2, nb, k, bs)

    col_source, row_source = pl.pallas_call(
        gather_kernel,
        out_shape=gathered,
        in_specs=[VMEM],
        out_specs=(ANY, ANY),
        scratch_shapes=gather_scratch,
        compiler_params=params(0),
    )(vectors)
    partials = products(block_values, block_rows, block_cols, block_counts, col_source, row_source)
    col_source, row_source, current = pl.pallas_call(
        middle_kernel,
        out_shape=gathered + (whole_vectors,),
        in_specs=[ANY, ANY, VMEM, SMEM, SMEM],
        out_specs=(ANY, ANY, VMEM),
        scratch_shapes=scatter_scratch(nb, k, bs) + gather_scratch,
        compiler_params=params(1),
    )(*apart(partials), vectors, center, radius)
    partials = products(block_values, block_rows, block_cols, block_counts, col_source, row_source)
    return pl.pallas_call(
        last_kernel,
        out_shape=whole_vectors,
        in_specs=[ANY, ANY, VMEM, VMEM, SMEM, SMEM],
        out_specs=VMEM,
        scratch_shapes=scatter_scratch(nb, k, bs),
        compiler_params=params(2),
    )(*apart(partials), current, vectors, center, radius)


def solution(mesh):
    return jax.shard_map(
        shards,
        mesh=mesh,
        in_specs=(
            P(None, ("row", "col")),
            P(("row", "col"), None, None),
            P(("row", "col")),
            P(("row", "col")),
            P(("row", "col")),
            P(),
            P(),
        ),
        out_specs=P(None, ("row", "col")),
        check_vma=False,
    )
```

```python
import functools

import jax
import jax.numpy as jnp
from jax import lax
from jax.experimental import pallas as pl
from jax.experimental.pallas import tpu as pltpu
from jax.sharding import PartitionSpec as P

MESH = pl.DeviceIdType.MESH
BF16, F32 = jnp.bfloat16, jnp.float32
ANY = pl.BlockSpec(memory_space=pl.ANY)
VMEM = pl.BlockSpec(memory_space=pltpu.VMEM)
SMEM = pl.BlockSpec(memory_space=pltpu.SMEM)
GATHER_COPIES, SCATTER_COPIES = 48, 32
UNROLL = 16


class Place:
    def __init__(self):
        row, col = lax.axis_index("row"), lax.axis_index("col")
        self.row, self.col = row, col
        self.y, self.z, self.c = row // 8, (row // 2) % 4, row % 2
        self.x, self.h = col // 2, col % 2
        z = self.z
        self.inner = (z == 1) | (z == 2)
        self.pair = z + 1 - 2 * (z % 2)
        self.near_z = 2 - z // 2
        self.far_z = 3 - 3 * (z // 2)

    def row_of(self, y=None, z=None, c=None):
        y = self.y if y is None else y
        z = self.z if z is None else z
        c = self.c if c is None else c
        return (y * 4 + z) * 2 + c

    def at_y(self, step):
        return (self.row_of(y=(self.y + step) % 4), self.col)

    def at_z(self, z):
        return (self.row_of(z=z), self.col)

    def at_x(self, step):
        return (self.row, ((self.x + step) % 4) * 2 + self.h)

    def other_core(self):
        return (self.row_of(c=1 - self.c), self.col)

    def across_z(self):
        return (self.row, self.x * 2 + 1 - self.h)

    def partners(self):
        z = self.z
        found = [self.other_core(), self.at_y(1), self.at_y(3), self.at_x(1), self.at_x(3)]
        found += [self.at_z(self.pair), self.at_z((z + 2) % 4), self.at_z(3 - z)]
        return found + [self.across_z()]


class Wire:
    def __init__(self, send_sems, recv_sems):
        self.send_sems, self.recv_sems = send_sems, recv_sems
        self.started, self.count = [], 0

    def slot(self):
        self.count += 1
        return self.count - 1

    def send(self, src, dst, device, recv=None, when=None):
        index = self.slot()
        copy = pltpu.make_async_remote_copy(
            src_ref=src,
            dst_ref=dst,
            send_sem=self.send_sems.at[index],
            recv_sem=self.recv_sems.at[index if recv is None else recv],
            device_id=device,
            device_id_type=MESH,
        )
        if when is None:
            copy.start()
        else:
            pl.when(when)(copy.start)
        self.started.append((copy, when))
        return copy

    def drain(self):
        for copy, when in self.started:
            if when is None:
                copy.wait_send()
            else:
                pl.when(when)(copy.wait_send)


def gather_parts(place, wire, cols_out, rows_out, nb, mirror_steps):
    hf = nb // 2
    y, z, c, x, h = place.y, place.z, place.c, place.x, place.h

    def cc(yy, zz, part=None):
        start, size = (0, nb) if part is None else (part * hf, hf)
        return cols_out.at[pl.ds(place.row_of(y=yy, z=zz) * nb + start, size)]

    def rr(xx, hh, part=None):
        start, size = (0, nb) if part is None else (part * hf, hf)
        return rows_out.at[pl.ds((xx * 2 + hh) * nb + start, size)]

    same = lambda ref, device, **kw: wire.send(ref, ref, device, **kw)
    mid, pair = place.at_z(3 - z), place.at_z(place.pair)
    order = [z, place.pair, place.near_z, place.far_z]
    ups, downs, rights, lefts, cores = [], [], [], [], []
    up_halves, down_halves, right_halves, left_halves = [], [], [], []

    def along_y(k):
        piece = cc(y, order[k])
        ups.append(same(piece, place.at_y(1)))
        downs.append(same(piece, place.at_y(3)))
        cores.append(same(piece, place.other_core()))

    def along_x(hh):
        rights.append(same(rr(x, hh), place.at_x(1)))
        lefts.append(same(rr(x, hh), place.at_x(3)))

    def forward_y(k):
        low, high = (y + 3) % 4, (y + 1) % 4
        ups[k].wait_recv()
        up_halves.append(same(cc(low, order[k], 0), place.at_y(1)))
        cores.append(same(cc(low, order[k]), place.other_core()))
        downs[k].wait_recv()
        down_halves.append(same(cc(high, order[k], 1), place.at_y(3)))
        cores.append(same(cc(high, order[k]), place.other_core()))

    def forward_x(k, hh):
        rights[k].wait_recv()
        right_halves.append(same(rr((x + 3) % 4, hh, 0), place.at_x(1)))
        lefts[k].wait_recv()
        left_halves.append(same(rr((x + 1) % 4, hh, 1), place.at_x(3)))

    def last_y(k):
        up_halves[k].wait_recv()
        down_halves[k].wait_recv()
        cores.append(same(cc((y + 2) % 4, order[k]), place.other_core()))

    mine, near_slot, far_slot = cc(y, z), wire.slot(), wire.slot()
    from_pair = same(mine, pair)
    from_near = same(mine, mid, recv=near_slot, when=place.inner)
    along_y(0)
    along_x(h)
    far = same(rr(x, h), place.across_z())
    from_pair.wait_recv()
    from_far = same(cc(y, place.pair), mid, recv=far_slot, when=place.inner)
    along_y(1)
    from_near.wait_recv()
    same(cc(y, place.near_z), pair, recv=near_slot, when=place.inner)
    along_y(2)
    forward_y(0)
    forward_x(0, h)
    from_far.wait_recv()
    same(cc(y, place.far_z), pair, recv=far_slot, when=place.inner)
    along_y(3)
    forward_y(1)
    far.wait_recv()
    along_x(1 - h)
    forward_x(1, 1 - h)
    forward_y(2)
    for copy in right_halves + left_halves:
        copy.wait_recv()
    mirror_steps[0]()
    forward_y(3)
    last_y(0)
    last_y(1)
    mirror_steps[1]()
    last_y(2)
    mirror_steps[2]()
    last_y(3)
    mirror_steps[3]()
    for copy in cores:
        copy.wait_recv()


def scatter_parts(place, wire, here, local, nb, last_of_col, last_of_row, forward_steps):
    ca, bp, bm, cp, cm, d, ep, em, gp, gm, v = here
    mirror_sums, forward_sums, mo, s, sf = local
    hf = nb // 2
    y, z, c, x, h = place.y, place.z, place.c, place.x, place.h
    order = [3 - z, (z + 2) % 4, place.pair, z]
    halves = [1 - h, h]
    first, last = pl.ds(0, hf), pl.ds(hf, hf)
    core_copies, y_first, y_second, x_first, x_second, z_copies = [], [], [], [], [], []

    def blocks(count, body):
        def step(b, carry):
            body(b)
            return carry

        lax.fori_loop(0, count, step, 0, unroll=4)

    def mirror_part(k, yy, core, b):
        return mirror_sums[last_of_col(((yy * 4 + order[k]) * 2 + core) * nb + b)]

    def add(target, addend):
        def body(b):
            target[b] = target[b] + addend[b]

        blocks(hf, body)

    def to_core(k):
        for yy in range(4):

            def body(b):
                mo[k, yy, b] = mirror_part(k, yy, 1 - c, b).astype(BF16)

            blocks(nb, body)
        core_copies.append(wire.send(mo.at[k], ca.at[k], place.other_core()))

    def own(k, yy):
        def body(b):
            s[k, yy, b] = (mirror_part(k, yy, c, b) + ca[k, yy, b].astype(F32)).astype(BF16)

        blocks(nb, body)

    def first_y(k):
        across = (y + 2) % 4
        core_copies[k].wait_recv()
        own(k, across)
        y_first.append((
            wire.send(s.at[k, across, first], bp.at[k], place.at_y(1)),
            wire.send(s.at[k, across, last], bm.at[k], place.at_y(3)),
        ))
        own(k, (y + 1) % 4)
        own(k, (y + 3) % 4)

    def second_y(k):
        y_first[k][0].wait_recv()
        add(s.at[k, (y + 1) % 4, first], bp.at[k])
        up = wire.send(s.at[k, (y + 1) % 4], cp.at[k], place.at_y(1))
        y_first[k][1].wait_recv()
        add(s.at[k, (y + 3) % 4, last], bm.at[k])
        y_second.append((up, wire.send(s.at[k, (y + 3) % 4], cm.at[k], place.at_y(3))))

    def home(k, b):
        total = mirror_part(k, y, c, b) + ca[k, y, b].astype(F32)
        return total + cp[k, b].astype(F32) + cm[k, b].astype(F32)

    def third(k):
        y_second[k][0].wait_recv()
        y_second[k][1].wait_recv()

        def body(b):
            s[k, y, b] = home(k, b).astype(BF16)

        blocks(nb, body)
        z_copies.append(wire.send(s.at[k, y], d.at[k], place.at_z(order[k])))

    def first_x(k):
        for xx in range(4):

            def body(b):
                sf[k, xx, b] = forward_sums[last_of_row((xx * 2 + halves[k]) * nb + b)].astype(BF16)

            blocks(nb, body)
        across = (x + 2) % 4
        x_first.append((
            wire.send(sf.at[k, across, first], ep.at[k], place.at_x(1)),
            wire.send(sf.at[k, across, last], em.at[k], place.at_x(3)),
        ))

    def second_x(k):
        x_first[k][0].wait_recv()
        add(sf.at[k, (x + 1) % 4, first], ep.at[k])
        right = wire.send(sf.at[k, (x + 1) % 4], gp.at[k], place.at_x(1))
        x_first[k][1].wait_recv()
        add(sf.at[k, (x + 3) % 4, last], em.at[k])
        x_second.append((right, wire.send(sf.at[k, (x + 3) % 4], gm.at[k], place.at_x(3))))

    def across_z():
        x_second[0][0].wait_recv()
        x_second[0][1].wait_recv()

        def body(b):
            total = sf[0, x, b].astype(F32) + gp[0, b].astype(F32) + gm[0, b].astype(F32)
            sf[0, x, b] = total.astype(BF16)

        blocks(nb, body)
        return wire.send(sf.at[0, x], v, place.across_z())

    for k in range(4):
        to_core(k)
    first_y(0)
    first_y(1)
    forward_steps[0]()
    second_y(0)
    first_y(2)
    forward_steps[1]()
    second_y(1)
    first_y(3)
    forward_steps[2]()
    second_y(2)
    third(0)
    forward_steps[3]()
    first_x(0)
    first_x(1)
    second_y(3)
    third(1)
    second_x(0)
    second_x(1)
    far = across_z()
    third(2)
    for copy in x_second[1] + y_second[3] + tuple(z_copies) + (far,):
        copy.wait_recv()

    def image(b):
        total = home(3, b)
        total = total + d[0, b].astype(F32) + d[1, b].astype(F32) + d[2, b].astype(F32)
        total = total + sf[1, x, b].astype(F32) + gp[1, b].astype(F32) + gm[1, b].astype(F32)
        return total + v[b].astype(F32)

    return image


REMOTE = 13


def filter_kernel(
    vectors, tables, center, radius, blocks_hbm, result, blocks, mirror_sums, forward_sums, mo, s, sf, current,
    *rest,
):
    place = Place()
    barrier = pltpu.get_barrier_semaphore()
    partners = place.partners()
    for partner in partners:
        pl.semaphore_signal(barrier, inc=1, device_id=partner, device_id_type=MESH)
    products = [rest[:REMOTE], rest[REMOTE : 2 * REMOTE]]
    gather_sems, scatter_sems, block_sem = rest[2 * REMOTE : 2 * REMOTE + 4], rest[2 * REMOTE + 4 : -1], rest[-1]
    capacity, bs = blocks.shape[0], blocks.shape[1]
    nb = vectors.shape[1] // bs
    col_total, row_total = products[0][0].shape[0], products[0][1].shape[0]
    fetch = pltpu.make_async_copy(blocks_hbm, blocks, block_sem)
    fetch.start()
    k = vectors.shape[0]
    mirror_sums[capacity] = jnp.zeros((k, bs), F32)
    forward_sums[capacity] = jnp.zeros((k, bs), F32)
    row_at = lambda i: tables[i]
    col_at = lambda i: tables[capacity + i]
    before_in_row = lambda i: tables[2 * capacity + i]
    before_in_col = lambda i: tables[3 * capacity + i]
    last_of_row = lambda i: tables[4 * capacity + i]
    last_of_col = lambda i: tables[4 * capacity + row_total + i]
    span = capacity // 4

    def steps(source, source_at, before, sums, contract):
        def part(first):
            def body(i, carry):
                start = first + i * UNROLL
                terms = [
                    lax.dot_general(
                        source[source_at(start + u)],
                        blocks[start + u],
                        (((1,), (contract,)), ((), ())),
                        preferred_element_type=F32,
                    )
                    for u in range(UNROLL)
                ]
                for u in range(UNROLL):
                    sums[start + u] = terms[u] + sums[before(start + u)]
                return carry

            lax.fori_loop(0, span // UNROLL, body, 0)

        return [functools.partial(part, i * span) for i in range(4)]

    def put_own(cols_out, rows_out, b, value):
        narrow = value.astype(BF16)
        cols_out[place.row * nb + b] = narrow
        rows_out[place.col * nb + b] = narrow

    for b in range(nb):
        put_own(products[0][0], products[0][1], b, vectors[:, b * bs : (b + 1) * bs])
    pl.semaphore_wait(barrier, len(partners))
    for p in range(2):
        cols_in, rows_in = products[p][:2]
        mirror_steps = steps(rows_in, row_at, before_in_col, mirror_sums, 0)
        forward_steps = steps(cols_in, col_at, before_in_row, forward_sums, 1)
        if p == 0:
            first_step = mirror_steps[0]

            def fetched(first_step=first_step):
                fetch.wait()
                first_step()

            mirror_steps[0] = fetched
        gather = Wire(gather_sems[2 * p], gather_sems[2 * p + 1])
        gather_parts(place, gather, cols_in, rows_in, nb, mirror_steps)
        scatter = Wire(scatter_sems[2 * p], scatter_sems[2 * p + 1])
        image = scatter_parts(
            place, scatter, products[p][2:], (mirror_sums, forward_sums, mo, s, sf), nb, last_of_col, last_of_row,
            forward_steps,
        )
        for b in range(nb):
            part = slice(b * bs, (b + 1) * bs)
            if p == 0:
                value = (image(b) - center[0] * vectors[:, part]) / radius[0]
                current[:, part] = value
                put_own(products[1][0], products[1][1], b, value)
            else:
                value = 2.0 * (image(b) - center[0] * current[:, part]) / radius[0] - vectors[:, part]
                result[:, part] = value
        gather.drain()
        scatter.drain()


def slot_tables(rows, cols, counts, row_total, col_total):
    capacity = rows.shape[0]
    slots = jnp.arange(capacity, dtype=jnp.int32)
    live = slots < counts[0]

    def latest(keys, queries, limits):
        hits = (keys[None, :] == queries[:, None]) & (slots[None, :] < limits[:, None]) & live[None, :]
        found = jnp.max(jnp.where(hits, slots[None, :], -1), axis=1)
        return jnp.where(found < 0, capacity, found)

    def whole(keys, total):
        return latest(keys, jnp.arange(total, dtype=jnp.int32), jnp.full((total,), capacity, jnp.int32))

    return jnp.concatenate([
        rows, cols, latest(rows, rows, slots), latest(cols, cols, slots), whole(rows, row_total), whole(cols, col_total)
    ])


def shards(vectors, block_values, block_rows, block_cols, block_counts, center, radius):
    k, own_rows = vectors.shape
    capacity, bs, _ = block_values.shape
    nb = own_rows // bs
    row_total = lax.axis_size("col") * nb
    col_total = lax.axis_size("row") * nb
    tables = slot_tables(block_rows, block_cols, block_counts, row_total, col_total)
    whole, half = (nb, k, bs), (nb // 2, k, bs)
    remote = [
        pltpu.VMEM((col_total, k, bs), BF16),
        pltpu.VMEM((row_total, k, bs), BF16),
        pltpu.VMEM((4, 4) + whole, BF16),
        pltpu.VMEM((4,) + half, BF16),
        pltpu.VMEM((4,) + half, BF16),
        pltpu.VMEM((4,) + whole, BF16),
        pltpu.VMEM((4,) + whole, BF16),
        pltpu.VMEM((3,) + whole, BF16),
        pltpu.VMEM((2,) + half, BF16),
        pltpu.VMEM((2,) + half, BF16),
        pltpu.VMEM((2,) + whole, BF16),
        pltpu.VMEM((2,) + whole, BF16),
        pltpu.VMEM(whole, BF16),
    ]
    return pl.pallas_call(
        filter_kernel,
        out_shape=jax.ShapeDtypeStruct((k, own_rows), F32),
        in_specs=[VMEM, SMEM, SMEM, SMEM, ANY],
        out_specs=VMEM,
        scratch_shapes=[
            pltpu.VMEM((capacity, bs, bs), BF16),
            pltpu.VMEM((capacity + 1, k, bs), F32),
            pltpu.VMEM((capacity + 1, k, bs), F32),
            pltpu.VMEM((4, 4) + whole, BF16),
            pltpu.VMEM((4, 4) + whole, BF16),
            pltpu.VMEM((2, 4) + whole, BF16),
            pltpu.VMEM((k, own_rows), F32),
        ]
        + remote * 2
        + [pltpu.SemaphoreType.DMA((GATHER_COPIES,))] * 4
        + [pltpu.SemaphoreType.DMA((SCATTER_COPIES,))] * 4
        + [pltpu.SemaphoreType.DMA],
        compiler_params=pltpu.CompilerParams(
            collective_id=0, has_side_effects=True, vmem_limit_bytes=56 * 2**20
        ),
        name="filter",
    )(vectors, tables, center, radius, block_values)


def solution(mesh):
    return jax.shard_map(
        shards,
        mesh=mesh,
        in_specs=(
            P(None, ("row", "col")),
            P(("row", "col"), None, None),
            P(("row", "col")),
            P(("row", "col")),
            P(("row", "col")),
            P(),
            P(),
        ),
        out_specs=P(None, ("row", "col")),
        check_vma=False,
    )
```

```python
import functools

import jax
import jax.numpy as jnp
from jax import lax
from jax.experimental import pallas as pl
from jax.experimental.pallas import tpu as pltpu
from jax.sharding import PartitionSpec as P

MESH = pl.DeviceIdType.MESH
BF16, F32 = jnp.bfloat16, jnp.float32
ANY = pl.BlockSpec(memory_space=pl.ANY)
VMEM = pl.BlockSpec(memory_space=pltpu.VMEM)
SMEM = pl.BlockSpec(memory_space=pltpu.SMEM)
COPIES, PARTS, UNROLL = 80, 4, 16


class Place:
    def __init__(self):
        row, col = lax.axis_index("row"), lax.axis_index("col")
        self.row, self.col = row, col
        self.y, self.z, self.c = row // 8, (row // 2) % 4, row % 2
        self.x, self.h = col // 2, col % 2
        z = self.z
        self.inner = (z == 1) | (z == 2)
        self.pair = z + 1 - 2 * (z % 2)
        self.near_z = 2 - z // 2
        self.far_z = 3 - 3 * (z // 2)

    def row_of(self, y=None, z=None, c=None):
        y = self.y if y is None else y
        z = self.z if z is None else z
        c = self.c if c is None else c
        return (y * 4 + z) * 2 + c

    def at_y(self, step):
        return (self.row_of(y=(self.y + step) % 4), self.col)

    def at_z(self, z):
        return (self.row_of(z=z), self.col)

    def at_x(self, step):
        return (self.row, ((self.x + step) % 4) * 2 + self.h)

    def other_core(self):
        return (self.row_of(c=1 - self.c), self.col)

    def across_z(self):
        return (self.row, self.x * 2 + 1 - self.h)

    def partners(self):
        z = self.z
        found = [self.other_core(), self.at_y(1), self.at_y(3), self.at_x(1), self.at_x(3)]
        found += [self.at_z(self.pair), self.at_z((z + 2) % 4), self.at_z(3 - z)]
        return found + [self.across_z()]


class Wire:
    def __init__(self, send_sems, recv_sems):
        self.send_sems, self.recv_sems = send_sems, recv_sems
        self.started, self.count = [], 0

    def slot(self):
        self.count += 1
        return self.count - 1

    def send(self, src, dst, device, recv=None, when=None):
        index = self.slot()
        copy = pltpu.make_async_remote_copy(
            src_ref=src,
            dst_ref=dst,
            send_sem=self.send_sems.at[index],
            recv_sem=self.recv_sems.at[index if recv is None else recv],
            device_id=device,
            device_id_type=MESH,
        )
        if when is None:
            copy.start()
        else:
            pl.when(when)(copy.start)
        self.started.append((copy, when))
        return copy

    def drain(self):
        for copy, when in self.started:
            if when is None:
                copy.wait_send()
            else:
                pl.when(when)(copy.wait_send)


SCRIPT = [
    "P", "N", "y0", "Z", "x0", "c0", "|", "wp", "F", "y1", "c1", "wn", "n>", "y2", "Y0", "X0", "wz", "x1",
    "c2", "C0", "wf", "f>", "y3", "Y1", "X1", "c3", "C1", "Y2", "C2", "H", "M0", "Y3", "C3", "M1", "L0", "D0",
    "L1", "D1", "M2", "L2", "D2", "M3", "A0", "A1", "A2", "A3", "B0", "B1", "L3", "D3", "B2", "B3", "K", "S0",
    "E0", "S1", "E1", "S2", "S3", "q0", "q1", "E2", "T0", "r0", "E3", "T1", "r1", "T2", "v", "W",
]


class Product:
    def __init__(self, place, wire, nb, remote, local, last_of_row, last_of_col, mirror_part, forward_part):
        self.place, self.wire, self.nb, self.hf = place, wire, nb, nb // 2
        self.cols, self.rows = remote[:2]
        self.ca, self.bp, self.bm, self.cp, self.cm, self.d, self.ep, self.em, self.gp, self.gm, self.v = remote[2:]
        self.mirror_sums, self.forward_sums, self.mo, self.s, self.sf = local
        self.last_of_row, self.last_of_col = last_of_row, last_of_col
        self.mirror_part, self.forward_part = mirror_part, forward_part
        self.near_slot, self.far_slot = wire.slot(), wire.slot()
        self.pieces = [place.z, place.pair, place.near_z, place.far_z]
        self.sums = [3 - place.z, (place.z + 2) % 4, place.pair, place.z]
        self.halves = [1 - place.h, place.h]
        self.made, self.cores = {}, []

    def run(self, codes):
        for code in codes:
            name, index = (code[:-1], int(code[-1])) if code[-1].isdigit() else (code, None)
            step = getattr(self, STEPS[name])
            step() if index is None else step(index)


    def cc(self, y, z, start=0, size=None):
        size = self.nb if size is None else size
        return self.cols.at[pl.ds(self.place.row_of(y=y, z=z) * self.nb + start, size)]

    def rr(self, x, h, start=0, size=None):
        size = self.nb if size is None else size
        return self.rows.at[pl.ds((x * 2 + h) * self.nb + start, size)]

    def same(self, key, ref, device, **options):
        self.made[key] = self.wire.send(ref, ref, device, **options)

    def arrived(self, *keys):
        for key in keys:
            self.made[key].wait_recv()

    def to_pair(self):
        self.same("pair", self.cc(self.place.y, self.place.z), self.place.at_z(self.place.pair))

    def to_middle(self):
        p = self.place
        self.same("near", self.cc(p.y, p.z), p.at_z(3 - p.z), recv=self.near_slot, when=p.inner)

    def pair_to_middle(self):
        p = self.place
        self.same("far", self.cc(p.y, p.pair), p.at_z(3 - p.z), recv=self.far_slot, when=p.inner)

    def near_to_pair(self):
        p = self.place
        self.same("near2", self.cc(p.y, p.near_z), p.at_z(p.pair), recv=self.near_slot, when=p.inner)

    def far_to_pair(self):
        p = self.place
        self.same("far2", self.cc(p.y, p.far_z), p.at_z(p.pair), recv=self.far_slot, when=p.inner)

    def wait_pair(self):
        self.arrived("pair")

    def wait_near(self):
        self.arrived("near")

    def wait_far(self):
        self.arrived("far")

    def along_y(self, k):
        p = self.place
        piece = self.cc(p.y, self.pieces[k])
        self.same(("up", k), piece, p.at_y(1))
        self.same(("down", k), piece, p.at_y(3))

    def core(self, y, k):
        piece = self.cc(y % 4, self.pieces[k])
        self.cores.append(self.wire.send(piece, piece, self.place.other_core()))

    def core_own(self, k):
        self.core(self.place.y, k)

    def core_next(self, k):
        self.core(self.place.y + 3, k)
        self.core(self.place.y + 1, k)

    def core_across(self, k):
        self.core(self.place.y + 2, k)

    def forward_y(self, k):
        p, hf = self.place, self.hf
        self.arrived(("up", k))
        self.same(("up half", k), self.cc((p.y + 3) % 4, self.pieces[k], 0, hf), p.at_y(1))
        self.arrived(("down", k))
        self.same(("down half", k), self.cc((p.y + 1) % 4, self.pieces[k], hf, hf), p.at_y(3))

    def wait_y(self, k):
        self.arrived(("up half", k), ("down half", k))

    def across(self):
        p = self.place
        self.same("z", self.rr(p.x, p.h), p.across_z())

    def wait_across(self):
        self.arrived("z")

    def along_x(self, i):
        p = self.place
        piece = self.rr(p.x, self.halves[1 - i])
        self.same(("right", i), piece, p.at_x(1))
        self.same(("left", i), piece, p.at_x(3))

    def forward_x(self, i):
        p, hf, h = self.place, self.hf, self.halves[1 - i]
        self.arrived(("right", i))
        self.same(("right half", i), self.rr((p.x + 3) % 4, h, 0, hf), p.at_x(1))
        self.arrived(("left", i))
        self.same(("left half", i), self.rr((p.x + 1) % 4, h, hf, hf), p.at_x(3))

    def wait_x(self):
        for i in range(2):
            self.arrived(("right half", i), ("left half", i))

    def wait_cores(self):
        for copy in self.cores:
            copy.wait_recv()


    def blocks(self, count, body):
        def step(b, carry):
            body(b)
            return carry

        lax.fori_loop(0, count, step, 0, unroll=4)

    def mirror_of(self, k, y, core, b):
        return self.mirror_sums[self.last_of_col(((y * 4 + self.sums[k]) * 2 + core) * self.nb + b)]

    def add(self, target, addend):
        def body(b):
            target[b] = target[b] + addend[b]

        self.blocks(self.hf, body)

    def send(self, key, src, dst, device):
        self.made[key] = self.wire.send(src, dst, device)

    def to_core(self, k):
        for y in range(4):

            def body(b):
                self.mo[k, y, b] = self.mirror_of(k, y, 1 - self.place.c, b).astype(BF16)

            self.blocks(self.nb, body)
        self.send(("core", k), self.mo.at[k], self.ca.at[k], self.place.other_core())

    def own(self, k, y):
        def body(b):
            mine = self.mirror_of(k, y, self.place.c, b)
            self.s[k, y, b] = (mine + self.ca[k, y, b].astype(F32)).astype(BF16)

        self.blocks(self.nb, body)

    def first_y(self, k):
        p, hf = self.place, self.hf
        across = (p.y + 2) % 4
        self.arrived(("core", k))
        self.own(k, across)
        self.send(("b up", k), self.s.at[k, across, pl.ds(0, hf)], self.bp.at[k], p.at_y(1))
        self.send(("b down", k), self.s.at[k, across, pl.ds(hf, hf)], self.bm.at[k], p.at_y(3))
        self.own(k, (p.y + 1) % 4)
        self.own(k, (p.y + 3) % 4)

    def second_y(self, k):
        p, hf = self.place, self.hf
        up, down = (p.y + 1) % 4, (p.y + 3) % 4
        self.arrived(("b up", k))
        self.add(self.s.at[k, up, pl.ds(0, hf)], self.bp.at[k])
        self.send(("c up", k), self.s.at[k, up], self.cp.at[k], p.at_y(1))
        self.arrived(("b down", k))
        self.add(self.s.at[k, down, pl.ds(hf, hf)], self.bm.at[k])
        self.send(("c down", k), self.s.at[k, down], self.cm.at[k], p.at_y(3))

    def home(self, k, b):
        total = self.mirror_of(k, self.place.y, self.place.c, b) + self.ca[k, self.place.y, b].astype(F32)
        return total + self.cp[k, b].astype(F32) + self.cm[k, b].astype(F32)

    def third_z(self, k):
        self.arrived(("c up", k), ("c down", k))
        target = self.s.at[k, self.place.y]

        def body(b):
            target[b] = self.home(k, b).astype(BF16)

        self.blocks(self.nb, body)
        self.send(("d", k), target, self.d.at[k], self.place.at_z(self.sums[k]))

    def first_x(self, k):
        p, hf = self.place, self.hf
        for x in range(4):

            def body(b):
                at = (x * 2 + self.halves[k]) * self.nb + b
                self.sf[k, x, b] = self.forward_sums[self.last_of_row(at)].astype(BF16)

            self.blocks(self.nb, body)
        across = (p.x + 2) % 4
        self.send(("e right", k), self.sf.at[k, across, pl.ds(0, hf)], self.ep.at[k], p.at_x(1))
        self.send(("e left", k), self.sf.at[k, across, pl.ds(hf, hf)], self.em.at[k], p.at_x(3))

    def second_x(self, k):
        p, hf = self.place, self.hf
        right, left = (p.x + 1) % 4, (p.x + 3) % 4
        self.arrived(("e right", k))
        self.add(self.sf.at[k, right, pl.ds(0, hf)], self.ep.at[k])
        self.send(("g right", k), self.sf.at[k, right], self.gp.at[k], p.at_x(1))
        self.arrived(("e left", k))
        self.add(self.sf.at[k, left, pl.ds(hf, hf)], self.em.at[k])
        self.send(("g left", k), self.sf.at[k, left], self.gm.at[k], p.at_x(3))

    def third_x(self):
        self.arrived(("g right", 0), ("g left", 0))
        target = self.sf.at[0, self.place.x]

        def body(b):
            total = target[b].astype(F32) + self.gp[0, b].astype(F32) + self.gm[0, b].astype(F32)
            target[b] = total.astype(BF16)

        self.blocks(self.nb, body)
        self.send("v", target, self.v, self.place.across_z())

    def wait_sums(self):
        self.arrived(("c up", 3), ("c down", 3), ("g right", 1), ("g left", 1))
        self.arrived(("d", 0), ("d", 1), ("d", 2), "v")

    def image(self, b):
        total = self.home(3, b)
        total = total + self.d[0, b].astype(F32) + self.d[1, b].astype(F32) + self.d[2, b].astype(F32)
        total = total + self.sf[1, self.place.x, b].astype(F32)
        total = total + self.gp[1, b].astype(F32) + self.gm[1, b].astype(F32)
        return total + self.v[b].astype(F32)


STEPS = dict(
    P="to_pair", N="to_middle", F="pair_to_middle", wp="wait_pair", wn="wait_near", wf="wait_far", y="along_y",
    c="core_own", C="core_next", D="core_across", Y="forward_y", L="wait_y", Z="across", wz="wait_across",
    x="along_x", X="forward_x", H="wait_x", K="wait_cores", M="mirror_part", S="forward_part", A="to_core",
    B="first_y", E="second_y", T="third_z", q="first_x", r="second_x", v="third_x", W="wait_sums",
)
STEPS["n>"], STEPS["f>"] = "near_to_pair", "far_to_pair"


REMOTE = 13


def filter_kernel(
    vectors, row_keys, col_keys, row_at, col_at, counts, center, radius, blocks_hbm, result,
    blocks, mirror_sums, forward_sums, mo, s, sf, current, found, tables, *rest,
):
    place = Place()
    barrier = pltpu.get_barrier_semaphore()
    partners = place.partners()
    for partner in partners:
        pl.semaphore_signal(barrier, inc=1, device_id=partner, device_id_type=MESH)
    products = [rest[:REMOTE], rest[REMOTE : 2 * REMOTE]]
    sems, block_sem, table_sem = rest[2 * REMOTE : -2], rest[-2], rest[-1]
    capacity, bs = blocks.shape[0], blocks.shape[1]
    nb = vectors.shape[1] // bs
    col_total, row_total = products[0][0].shape[0], products[0][1].shape[0]
    fetch = pltpu.make_async_copy(blocks_hbm, blocks, block_sem)
    fetch.start()
    k = vectors.shape[0]
    mirror_sums[capacity] = jnp.zeros((k, bs), F32)
    forward_sums[capacity] = jnp.zeros((k, bs), F32)
    before_in_row = lambda i: tables[0, i]
    before_in_col = lambda i: tables[0, capacity + i]
    last_of_row = lambda i: tables[0, 2 * capacity + i]
    last_of_col = lambda i: tables[0, 2 * capacity + row_total + i]
    span = capacity // PARTS

    def part_of(source, source_at, before, sums, contract):
        def part(index):
            first = index * span

            def body(i, carry):
                start = first + i * UNROLL
                terms = [
                    lax.dot_general(
                        source[source_at[start + u]],
                        blocks[start + u],
                        (((1,), (contract,)), ((), ())),
                        preferred_element_type=F32,
                    )
                    for u in range(UNROLL)
                ]
                for u in range(UNROLL):
                    sums[start + u] = terms[u] + sums[before(start + u)]
                return carry

            lax.fori_loop(0, span // UNROLL, body, 0)

        return part

    def put_own(cols_out, rows_out, b, value):
        narrow = value.astype(BF16)
        cols_out[place.row * nb + b] = narrow
        rows_out[place.col * nb + b] = narrow

    def make_tables():
        square = (capacity, capacity)
        down, along = lax.broadcasted_iota(jnp.int32, square, 0), lax.broadcasted_iota(jnp.int32, square, 1)
        count = counts[0]
        offset = 0

        def store(hits, size):
            nonlocal offset
            slots = lax.broadcasted_iota(jnp.int32, (capacity, size), 0)
            latest = jnp.max(jnp.where(hits, slots, -1), axis=0, keepdims=True)
            found[:, offset : offset + size] = jnp.where(latest < 0, capacity, latest)
            offset += size

        keys_down = []
        for keys in (row_keys, col_keys):
            spread = jnp.broadcast_to(keys[...], square)
            down_keys = jnp.sum(jnp.where(down == along, spread, 0), axis=1, keepdims=True)
            keys_down.append(down_keys)
            store((down_keys == spread) & (down < along) & (down < count), capacity)
        for down_keys, total in zip(keys_down, (row_total, col_total)):
            wanted = lax.broadcasted_iota(jnp.int32, (capacity, total), 1)
            live = lax.broadcasted_iota(jnp.int32, (capacity, total), 0) < count
            store((down_keys == wanted) & live, total)
        copy = pltpu.make_async_copy(found, tables, table_sem)
        copy.start()
        copy.wait()

    for b in range(nb):
        put_own(products[0][0], products[0][1], b, vectors[:, b * bs : (b + 1) * bs])
    pl.semaphore_wait(barrier, len(partners))
    for p in range(2):
        mirror_part = part_of(products[p][1], row_at, before_in_col, mirror_sums, 0)
        forward_part = part_of(products[p][0], col_at, before_in_row, forward_sums, 1)
        wire = Wire(sems[2 * p], sems[2 * p + 1])
        product = Product(
            place, wire, nb, products[p], (mirror_sums, forward_sums, mo, s, sf), last_of_row, last_of_col,
            mirror_part, forward_part,
        )
        tables_at = SCRIPT.index("|")
        product.run(SCRIPT[:tables_at])
        if p == 0:
            make_tables()
            fetch.wait()
        product.run(SCRIPT[tables_at + 1 :])
        for b in range(nb):
            part = slice(b * bs, (b + 1) * bs)
            if p == 0:
                value = (product.image(b) - center[0] * vectors[:, part]) / radius[0]
                current[:, part] = value
                put_own(products[1][0], products[1][1], b, value)
            else:
                value = 2.0 * (product.image(b) - center[0] * current[:, part]) / radius[0] - vectors[:, part]
                result[:, part] = value
        wire.drain()


def shards(vectors, block_values, block_rows, block_cols, block_counts, center, radius):
    k, own_rows = vectors.shape
    capacity, bs, _ = block_values.shape
    nb = own_rows // bs
    row_total = lax.axis_size("col") * nb
    col_total = lax.axis_size("row") * nb
    whole, half = (nb, k, bs), (nb // 2, k, bs)
    remote = [
        pltpu.VMEM((col_total, k, bs), BF16),
        pltpu.VMEM((row_total, k, bs), BF16),
        pltpu.VMEM((4, 4) + whole, BF16),
        pltpu.VMEM((4,) + half, BF16),
        pltpu.VMEM((4,) + half, BF16),
        pltpu.VMEM((4,) + whole, BF16),
        pltpu.VMEM((4,) + whole, BF16),
        pltpu.VMEM((3,) + whole, BF16),
        pltpu.VMEM((2,) + half, BF16),
        pltpu.VMEM((2,) + half, BF16),
        pltpu.VMEM((2,) + whole, BF16),
        pltpu.VMEM((2,) + whole, BF16),
        pltpu.VMEM(whole, BF16),
    ]
    return pl.pallas_call(
        filter_kernel,
        out_shape=jax.ShapeDtypeStruct((k, own_rows), F32),
        in_specs=[VMEM, VMEM, VMEM, SMEM, SMEM, SMEM, SMEM, SMEM, ANY],
        out_specs=VMEM,
        scratch_shapes=[
            pltpu.VMEM((capacity, bs, bs), BF16),
            pltpu.VMEM((capacity + 1, k, bs), F32),
            pltpu.VMEM((capacity + 1, k, bs), F32),
            pltpu.VMEM((4, 4) + whole, BF16),
            pltpu.VMEM((4, 4) + whole, BF16),
            pltpu.VMEM((2, 4) + whole, BF16),
            pltpu.VMEM((k, own_rows), F32),
            pltpu.VMEM((1, 2 * capacity + row_total + col_total), jnp.int32),
            pltpu.SMEM((1, 2 * capacity + row_total + col_total), jnp.int32),
        ]
        + remote * 2
        + [pltpu.SemaphoreType.DMA((COPIES,))] * 4
        + [pltpu.SemaphoreType.DMA] * 2,
        compiler_params=pltpu.CompilerParams(
            collective_id=0, has_side_effects=True, vmem_limit_bytes=56 * 2**20
        ),
        name="filter",
    )(
        vectors, block_rows.reshape(1, capacity), block_cols.reshape(1, capacity), block_rows, block_cols,
        block_counts, center, radius, block_values,
    )


def solution(mesh):
    return jax.shard_map(
        shards,
        mesh=mesh,
        in_specs=(
            P(None, ("row", "col")),
            P(("row", "col"), None, None),
            P(("row", "col")),
            P(("row", "col")),
            P(("row", "col")),
            P(),
            P(),
        ),
        out_specs=P(None, ("row", "col")),
        check_vma=False,
    )
```

```python
import functools

import jax
import jax.numpy as jnp
from jax import lax
from jax.experimental import pallas as pl
from jax.experimental.pallas import tpu as pltpu
from jax.sharding import PartitionSpec as P

MESH = pl.DeviceIdType.MESH
BF16, F32 = jnp.bfloat16, jnp.float32
ANY = pl.BlockSpec(memory_space=pl.ANY)
VMEM = pl.BlockSpec(memory_space=pltpu.VMEM)
SMEM = pl.BlockSpec(memory_space=pltpu.SMEM)
COPIES, PARTS, UNROLL = 80, 4, 32


class Place:
    def __init__(self):
        row, col = lax.axis_index("row"), lax.axis_index("col")
        self.row, self.col = row, col
        self.y, self.z, self.c = row // 8, (row // 2) % 4, row % 2
        self.x, self.h = col // 2, col % 2
        z = self.z
        self.inner = (z == 1) | (z == 2)
        self.pair = z + 1 - 2 * (z % 2)
        self.near_z = 2 - z // 2
        self.far_z = 3 - 3 * (z // 2)

    def row_of(self, y=None, z=None, c=None):
        y = self.y if y is None else y
        z = self.z if z is None else z
        c = self.c if c is None else c
        return (y * 4 + z) * 2 + c

    def at_y(self, step):
        return (self.row_of(y=(self.y + step) % 4), self.col)

    def at_z(self, z):
        return (self.row_of(z=z), self.col)

    def at_x(self, step):
        return (self.row, ((self.x + step) % 4) * 2 + self.h)

    def other_core(self):
        return (self.row_of(c=1 - self.c), self.col)

    def across_z(self):
        return (self.row, self.x * 2 + 1 - self.h)

    def partners(self):
        z = self.z
        found = [self.other_core(), self.at_y(1), self.at_y(3), self.at_x(1), self.at_x(3)]
        found += [self.at_z(self.pair), self.at_z((z + 2) % 4), self.at_z(3 - z)]
        return found + [self.across_z()]


class Wire:
    def __init__(self, send_sems, recv_sems):
        self.send_sems, self.recv_sems = send_sems, recv_sems
        self.started, self.count = [], 0

    def slot(self):
        self.count += 1
        return self.count - 1

    def send(self, src, dst, device, recv=None, when=None):
        index = self.slot()
        copy = pltpu.make_async_remote_copy(
            src_ref=src,
            dst_ref=dst,
            send_sem=self.send_sems.at[index],
            recv_sem=self.recv_sems.at[index if recv is None else recv],
            device_id=device,
            device_id_type=MESH,
        )
        if when is None:
            copy.start()
        else:
            pl.when(when)(copy.start)
        self.started.append((copy, when))
        return copy

    def drain(self):
        for copy, when in self.started:
            if when is None:
                copy.wait_send()
            else:
                pl.when(when)(copy.wait_send)


SCRIPT = [
    "P", "N", "y0", "Z", "x0", "c0", "|", "wp", "F", "y1", "c1", "wn", "n>", "y2", "Y0", "X0", "wz", "x1",
    "c2", "C0", "wf", "f>", "y3", "Y1", "X1", "c3", "C1", "Y2", "C2", "H", "M0", "Y3", "C3", "M1", "L0", "D0",
    "L1", "D1", "M2", "L2", "D2", "M3", "A0", "A1", "A2", "A3", "B0", "B1", "L3", "D3", "B2", "B3", "K", "E0",
    "S0", "E1", "S1", "S2", "T0", "E2", "S3", "q0", "q1", "T1", "E3", "r0", "T2", "r1", "v", "W",
]


class Product:
    def __init__(self, place, wire, nb, remote, local, last_of_row, last_of_col, mirror_part, forward_part):
        self.place, self.wire, self.nb, self.hf = place, wire, nb, nb // 2
        self.cols, self.rows = remote[:2]
        self.ca, self.bp, self.bm, self.cp, self.cm, self.d, self.ep, self.em, self.gp, self.gm, self.v = remote[2:]
        self.mirror_sums, self.forward_sums, self.mo, self.s, self.sf = local
        self.last_of_row, self.last_of_col = last_of_row, last_of_col
        self.mirror_part, self.forward_part = mirror_part, forward_part
        self.near_slot, self.far_slot = wire.slot(), wire.slot()
        self.pieces = [place.z, place.pair, place.near_z, place.far_z]
        self.sums = [3 - place.z, (place.z + 2) % 4, place.pair, place.z]
        self.halves = [1 - place.h, place.h]
        self.made, self.cores = {}, []

    def run(self, codes):
        for code in codes:
            name, index = (code[:-1], int(code[-1])) if code[-1].isdigit() else (code, None)
            step = getattr(self, STEPS[name])
            step() if index is None else step(index)


    def cc(self, y, z, start=0, size=None):
        size = self.nb if size is None else size
        return self.cols.at[pl.ds(self.place.row_of(y=y, z=z) * self.nb + start, size)]

    def rr(self, x, h, start=0, size=None):
        size = self.nb if size is None else size
        return self.rows.at[pl.ds((x * 2 + h) * self.nb + start, size)]

    def same(self, key, ref, device, **options):
        self.made[key] = self.wire.send(ref, ref, device, **options)

    def arrived(self, *keys):
        for key in keys:
            self.made[key].wait_recv()

    def to_pair(self):
        self.same("pair", self.cc(self.place.y, self.place.z), self.place.at_z(self.place.pair))

    def to_middle(self):
        p = self.place
        self.same("near", self.cc(p.y, p.z), p.at_z(3 - p.z), recv=self.near_slot, when=p.inner)

    def pair_to_middle(self):
        p = self.place
        self.same("far", self.cc(p.y, p.pair), p.at_z(3 - p.z), recv=self.far_slot, when=p.inner)

    def near_to_pair(self):
        p = self.place
        self.same("near2", self.cc(p.y, p.near_z), p.at_z(p.pair), recv=self.near_slot, when=p.inner)

    def far_to_pair(self):
        p = self.place
        self.same("far2", self.cc(p.y, p.far_z), p.at_z(p.pair), recv=self.far_slot, when=p.inner)

    def wait_pair(self):
        self.arrived("pair")

    def wait_near(self):
        self.arrived("near")

    def wait_far(self):
        self.arrived("far")

    def along_y(self, k):
        p = self.place
        piece = self.cc(p.y, self.pieces[k])
        self.same(("up", k), piece, p.at_y(1))
        self.same(("down", k), piece, p.at_y(3))

    def core(self, y, k):
        piece = self.cc(y % 4, self.pieces[k])
        self.cores.append(self.wire.send(piece, piece, self.place.other_core()))

    def core_own(self, k):
        self.core(self.place.y, k)

    def core_next(self, k):
        self.core(self.place.y + 3, k)
        self.core(self.place.y + 1, k)

    def core_across(self, k):
        self.core(self.place.y + 2, k)

    def forward_y(self, k):
        p, hf = self.place, self.hf
        self.arrived(("up", k))
        self.same(("up half", k), self.cc((p.y + 3) % 4, self.pieces[k], 0, hf), p.at_y(1))
        self.arrived(("down", k))
        self.same(("down half", k), self.cc((p.y + 1) % 4, self.pieces[k], hf, hf), p.at_y(3))

    def wait_y(self, k):
        self.arrived(("up half", k), ("down half", k))

    def across(self):
        p = self.place
        self.same("z", self.rr(p.x, p.h), p.across_z())

    def wait_across(self):
        self.arrived("z")

    def along_x(self, i):
        p = self.place
        piece = self.rr(p.x, self.halves[1 - i])
        self.same(("right", i), piece, p.at_x(1))
        self.same(("left", i), piece, p.at_x(3))

    def forward_x(self, i):
        p, hf, h = self.place, self.hf, self.halves[1 - i]
        self.arrived(("right", i))
        self.same(("right half", i), self.rr((p.x + 3) % 4, h, 0, hf), p.at_x(1))
        self.arrived(("left", i))
        self.same(("left half", i), self.rr((p.x + 1) % 4, h, hf, hf), p.at_x(3))

    def wait_x(self):
        for i in range(2):
            self.arrived(("right half", i), ("left half", i))

    def wait_cores(self):
        for copy in self.cores:
            copy.wait_recv()


    def blocks(self, count, body):
        def step(b, carry):
            body(b)
            return carry

        lax.fori_loop(0, count, step, 0, unroll=4)

    def mirror_of(self, k, y, core, b):
        return self.mirror_sums[self.last_of_col(((y * 4 + self.sums[k]) * 2 + core) * self.nb + b)]

    def add(self, target, addend):
        def body(b):
            target[b] = target[b] + addend[b]

        self.blocks(self.hf, body)

    def send(self, key, src, dst, device):
        self.made[key] = self.wire.send(src, dst, device)

    def to_core(self, k):
        for y in range(4):

            def body(b):
                self.mo[k, y, b] = self.mirror_of(k, y, 1 - self.place.c, b).astype(BF16)

            self.blocks(self.nb, body)
        self.send(("core", k), self.mo.at[k], self.ca.at[k], self.place.other_core())

    def own(self, k, y):
        def body(b):
            mine = self.mirror_of(k, y, self.place.c, b)
            self.s[k, y, b] = (mine + self.ca[k, y, b].astype(F32)).astype(BF16)

        self.blocks(self.nb, body)

    def first_y(self, k):
        p, hf = self.place, self.hf
        across = (p.y + 2) % 4
        self.arrived(("core", k))
        self.own(k, across)
        self.send(("b up", k), self.s.at[k, across, pl.ds(0, hf)], self.bp.at[k], p.at_y(1))
        self.send(("b down", k), self.s.at[k, across, pl.ds(hf, hf)], self.bm.at[k], p.at_y(3))
        self.own(k, (p.y + 1) % 4)
        self.own(k, (p.y + 3) % 4)

    def second_y(self, k):
        p, hf = self.place, self.hf
        up, down = (p.y + 1) % 4, (p.y + 3) % 4
        self.arrived(("b up", k))
        self.add(self.s.at[k, up, pl.ds(0, hf)], self.bp.at[k])
        self.send(("c up", k), self.s.at[k, up], self.cp.at[k], p.at_y(1))
        self.arrived(("b down", k))
        self.add(self.s.at[k, down, pl.ds(hf, hf)], self.bm.at[k])
        self.send(("c down", k), self.s.at[k, down], self.cm.at[k], p.at_y(3))

    def home(self, k, b):
        total = self.mirror_of(k, self.place.y, self.place.c, b) + self.ca[k, self.place.y, b].astype(F32)
        return total + self.cp[k, b].astype(F32) + self.cm[k, b].astype(F32)

    def third_z(self, k):
        self.arrived(("c up", k), ("c down", k))
        target = self.s.at[k, self.place.y]

        def body(b):
            target[b] = self.home(k, b).astype(BF16)

        self.blocks(self.nb, body)
        self.send(("d", k), target, self.d.at[k], self.place.at_z(self.sums[k]))

    def first_x(self, k):
        p, hf = self.place, self.hf
        for x in range(4):

            def body(b):
                at = (x * 2 + self.halves[k]) * self.nb + b
                self.sf[k, x, b] = self.forward_sums[self.last_of_row(at)].astype(BF16)

            self.blocks(self.nb, body)
        across = (p.x + 2) % 4
        self.send(("e right", k), self.sf.at[k, across, pl.ds(0, hf)], self.ep.at[k], p.at_x(1))
        self.send(("e left", k), self.sf.at[k, across, pl.ds(hf, hf)], self.em.at[k], p.at_x(3))

    def second_x(self, k):
        p, hf = self.place, self.hf
        right, left = (p.x + 1) % 4, (p.x + 3) % 4
        self.arrived(("e right", k))
        self.add(self.sf.at[k, right, pl.ds(0, hf)], self.ep.at[k])
        self.send(("g right", k), self.sf.at[k, right], self.gp.at[k], p.at_x(1))
        self.arrived(("e left", k))
        self.add(self.sf.at[k, left, pl.ds(hf, hf)], self.em.at[k])
        self.send(("g left", k), self.sf.at[k, left], self.gm.at[k], p.at_x(3))

    def third_x(self):
        self.arrived(("g right", 0), ("g left", 0))
        target = self.sf.at[0, self.place.x]

        def body(b):
            total = target[b].astype(F32) + self.gp[0, b].astype(F32) + self.gm[0, b].astype(F32)
            target[b] = total.astype(BF16)

        self.blocks(self.nb, body)
        self.send("v", target, self.v, self.place.across_z())

    def wait_sums(self):
        self.arrived(("c up", 3), ("c down", 3), ("g right", 1), ("g left", 1))
        self.arrived(("d", 0), ("d", 1), ("d", 2), "v")

    def image(self, b):
        total = self.home(3, b)
        total = total + self.d[0, b].astype(F32) + self.d[1, b].astype(F32) + self.d[2, b].astype(F32)
        total = total + self.sf[1, self.place.x, b].astype(F32)
        total = total + self.gp[1, b].astype(F32) + self.gm[1, b].astype(F32)
        return total + self.v[b].astype(F32)


STEPS = dict(
    P="to_pair", N="to_middle", F="pair_to_middle", wp="wait_pair", wn="wait_near", wf="wait_far", y="along_y",
    c="core_own", C="core_next", D="core_across", Y="forward_y", L="wait_y", Z="across", wz="wait_across",
    x="along_x", X="forward_x", H="wait_x", K="wait_cores", M="mirror_part", S="forward_part", A="to_core",
    B="first_y", E="second_y", T="third_z", q="first_x", r="second_x", v="third_x", W="wait_sums",
)
STEPS["n>"], STEPS["f>"] = "near_to_pair", "far_to_pair"


REMOTE = 13


def filter_kernel(
    vectors, row_keys, col_keys, row_at, col_at, counts, center, radius, blocks_hbm, result,
    blocks, mirror_sums, forward_sums, mo, s, sf, current, found, tables, *rest,
):
    place = Place()
    barrier = pltpu.get_barrier_semaphore()
    partners = place.partners()
    for partner in partners:
        pl.semaphore_signal(barrier, inc=1, device_id=partner, device_id_type=MESH)
    products = [rest[:REMOTE], rest[REMOTE : 2 * REMOTE]]
    sems, block_sem, table_sem = rest[2 * REMOTE : -2], rest[-2], rest[-1]
    capacity, bs = blocks.shape[0], blocks.shape[1]
    nb = vectors.shape[1] // bs
    col_total, row_total = products[0][0].shape[0], products[0][1].shape[0]
    fetch = pltpu.make_async_copy(blocks_hbm, blocks, block_sem)
    fetch.start()
    k = vectors.shape[0]
    mirror_sums[capacity] = jnp.zeros((k, bs), F32)
    forward_sums[capacity] = jnp.zeros((k, bs), F32)
    before_in_row = lambda i: tables[0, i]
    before_in_col = lambda i: tables[0, capacity + i]
    last_of_row = lambda i: tables[0, 2 * capacity + i]
    last_of_col = lambda i: tables[0, 2 * capacity + row_total + i]
    span = capacity // PARTS

    def part_of(source, source_at, before, sums, contract):
        def part(index):
            first = index * span

            def body(i, carry):
                start = first + i * UNROLL
                terms = [
                    lax.dot_general(
                        source[source_at[start + u]],
                        blocks[start + u],
                        (((1,), (contract,)), ((), ())),
                        preferred_element_type=F32,
                    )
                    for u in range(UNROLL)
                ]
                for u in range(UNROLL):
                    sums[start + u] = terms[u] + sums[before(start + u)]
                return carry

            lax.fori_loop(0, span // UNROLL, body, 0)

        return part

    def put_own(cols_out, rows_out, b, value):
        narrow = value.astype(BF16)
        cols_out[place.row * nb + b] = narrow
        rows_out[place.col * nb + b] = narrow

    def make_tables():
        square = (capacity, capacity)
        down, along = lax.broadcasted_iota(jnp.int32, square, 0), lax.broadcasted_iota(jnp.int32, square, 1)
        count = counts[0]
        offset = 0

        def store(hits, size):
            nonlocal offset
            slots = lax.broadcasted_iota(jnp.int32, (capacity, size), 0)
            latest = jnp.max(jnp.where(hits, slots, -1), axis=0, keepdims=True)
            found[:, offset : offset + size] = jnp.where(latest < 0, capacity, latest)
            offset += size

        keys_down = []
        for keys in (row_keys, col_keys):
            spread = jnp.broadcast_to(keys[...], square)
            down_keys = jnp.sum(jnp.where(down == along, spread, 0), axis=1, keepdims=True)
            keys_down.append(down_keys)
            store((down_keys == spread) & (down < along) & (down < count), capacity)
        for down_keys, total in zip(keys_down, (row_total, col_total)):
            wanted = lax.broadcasted_iota(jnp.int32, (capacity, total), 1)
            live = lax.broadcasted_iota(jnp.int32, (capacity, total), 0) < count
            store((down_keys == wanted) & live, total)
        copy = pltpu.make_async_copy(found, tables, table_sem)
        copy.start()
        copy.wait()

    for b in range(nb):
        put_own(products[0][0], products[0][1], b, vectors[:, b * bs : (b + 1) * bs])
    pl.semaphore_wait(barrier, len(partners))
    for p in range(2):
        mirror_part = part_of(products[p][1], row_at, before_in_col, mirror_sums, 0)
        forward_part = part_of(products[p][0], col_at, before_in_row, forward_sums, 1)
        wire = Wire(sems[2 * p], sems[2 * p + 1])
        product = Product(
            place, wire, nb, products[p], (mirror_sums, forward_sums, mo, s, sf), last_of_row, last_of_col,
            mirror_part, forward_part,
        )
        tables_at = SCRIPT.index("|")
        product.run(SCRIPT[:tables_at])
        if p == 0:
            make_tables()
            fetch.wait()
        product.run(SCRIPT[tables_at + 1 :])
        for b in range(nb):
            part = slice(b * bs, (b + 1) * bs)
            if p == 0:
                value = (product.image(b) - center[0] * vectors[:, part]) / radius[0]
                current[:, part] = value
                put_own(products[1][0], products[1][1], b, value)
            else:
                value = 2.0 * (product.image(b) - center[0] * current[:, part]) / radius[0] - vectors[:, part]
                result[:, part] = value
        wire.drain()


def shards(vectors, block_values, block_rows, block_cols, block_counts, center, radius):
    k, own_rows = vectors.shape
    capacity, bs, _ = block_values.shape
    nb = own_rows // bs
    row_total = lax.axis_size("col") * nb
    col_total = lax.axis_size("row") * nb
    whole, half = (nb, k, bs), (nb // 2, k, bs)
    remote = [
        pltpu.VMEM((col_total, k, bs), BF16),
        pltpu.VMEM((row_total, k, bs), BF16),
        pltpu.VMEM((4, 4) + whole, BF16),
        pltpu.VMEM((4,) + half, BF16),
        pltpu.VMEM((4,) + half, BF16),
        pltpu.VMEM((4,) + whole, BF16),
        pltpu.VMEM((4,) + whole, BF16),
        pltpu.VMEM((3,) + whole, BF16),
        pltpu.VMEM((2,) + half, BF16),
        pltpu.VMEM((2,) + half, BF16),
        pltpu.VMEM((2,) + whole, BF16),
        pltpu.VMEM((2,) + whole, BF16),
        pltpu.VMEM(whole, BF16),
    ]
    return pl.pallas_call(
        filter_kernel,
        out_shape=jax.ShapeDtypeStruct((k, own_rows), F32),
        in_specs=[VMEM, VMEM, VMEM, SMEM, SMEM, SMEM, SMEM, SMEM, ANY],
        out_specs=VMEM,
        scratch_shapes=[
            pltpu.VMEM((capacity, bs, bs), BF16),
            pltpu.VMEM((capacity + 1, k, bs), F32),
            pltpu.VMEM((capacity + 1, k, bs), F32),
            pltpu.VMEM((4, 4) + whole, BF16),
            pltpu.VMEM((4, 4) + whole, BF16),
            pltpu.VMEM((2, 4) + whole, BF16),
            pltpu.VMEM((k, own_rows), F32),
            pltpu.VMEM((1, 2 * capacity + row_total + col_total), jnp.int32),
            pltpu.SMEM((1, 2 * capacity + row_total + col_total), jnp.int32),
        ]
        + remote * 2
        + [pltpu.SemaphoreType.DMA((COPIES,))] * 4
        + [pltpu.SemaphoreType.DMA] * 2,
        compiler_params=pltpu.CompilerParams(
            collective_id=0, has_side_effects=True, vmem_limit_bytes=56 * 2**20
        ),
        name="filter",
    )(
        vectors, block_rows.reshape(1, capacity), block_cols.reshape(1, capacity), block_rows, block_cols,
        block_counts, center, radius, block_values,
    )


def solution(mesh):
    return jax.shard_map(
        shards,
        mesh=mesh,
        in_specs=(
            P(None, ("row", "col")),
            P(("row", "col"), None, None),
            P(("row", "col")),
            P(("row", "col")),
            P(("row", "col")),
            P(),
            P(),
        ),
        out_specs=P(None, ("row", "col")),
        check_vma=False,
    )
```

```python
import functools

import jax
import jax.numpy as jnp
from jax import lax
from jax.experimental import pallas as pl
from jax.experimental.pallas import tpu as pltpu
from jax.sharding import PartitionSpec as P

MESH = pl.DeviceIdType.MESH
BF16, F32 = jnp.bfloat16, jnp.float32
ANY = pl.BlockSpec(memory_space=pl.ANY)
VMEM = pl.BlockSpec(memory_space=pltpu.VMEM)
SMEM = pl.BlockSpec(memory_space=pltpu.SMEM)
COPIES, PARTS, UNROLL = 80, 4, 32


class Place:
    def __init__(self):
        row, col = lax.axis_index("row"), lax.axis_index("col")
        self.row, self.col = row, col
        self.y, self.z, self.c = row // 8, (row // 2) % 4, row % 2
        self.x, self.h = col // 2, col % 2
        z = self.z
        self.inner = (z == 1) | (z == 2)
        self.pair = z + 1 - 2 * (z % 2)
        self.near_z = 2 - z // 2
        self.far_z = 3 - 3 * (z // 2)

    def row_of(self, y=None, z=None, c=None):
        y = self.y if y is None else y
        z = self.z if z is None else z
        c = self.c if c is None else c
        return (y * 4 + z) * 2 + c

    def at_y(self, step):
        return (self.row_of(y=(self.y + step) % 4), self.col)

    def at_z(self, z):
        return (self.row_of(z=z), self.col)

    def at_x(self, step):
        return (self.row, ((self.x + step) % 4) * 2 + self.h)

    def other_core(self):
        return (self.row_of(c=1 - self.c), self.col)

    def across_z(self):
        return (self.row, self.x * 2 + 1 - self.h)

    def partners(self):
        z = self.z
        found = [self.other_core(), self.at_y(1), self.at_y(3), self.at_x(1), self.at_x(3)]
        found += [self.at_z(self.pair), self.at_z((z + 2) % 4), self.at_z(3 - z)]
        return found + [self.across_z()]


class Wire:
    def __init__(self, send_sems, recv_sems):
        self.send_sems, self.recv_sems = send_sems, recv_sems
        self.started, self.count = [], 0

    def slot(self):
        self.count += 1
        return self.count - 1

    def send(self, src, dst, device, recv=None, when=None):
        index = self.slot()
        copy = pltpu.make_async_remote_copy(
            src_ref=src,
            dst_ref=dst,
            send_sem=self.send_sems.at[index],
            recv_sem=self.recv_sems.at[index if recv is None else recv],
            device_id=device,
            device_id_type=MESH,
        )
        if when is None:
            copy.start()
        else:
            pl.when(when)(copy.start)
        self.started.append((copy, when))
        return copy

    def drain(self):
        for copy, when in self.started:
            if when is None:
                copy.wait_send()
            else:
                pl.when(when)(copy.wait_send)


SCRIPT = [
    "P", "N", "y0", "Z", "x0", "c0", "|", "wp", "F", "y1", "c1", "wn", "n>", "y2", "Y0", "X0", "wz", "x1",
    "c2", "C0", "wf", "f>", "y3", "Y1", "X1", "c3", "C1", "Y2", "C2", "H", "M0", "Y3", "C3", "M1", "L0", "D0",
    "L1", "D1", "M2", "L2", "D2", "M3", "A0", "A1", "A2", "A3", "B0", "B1", "L3", "D3", "B2", "B3", "K", "S0",
    "E0", "S1", "E1", "S2", "S3", "q0", "q1", "E2", "T0", "r0", "E3", "T1", "r1", "T2", "v", "W",
]


class Product:
    def __init__(self, place, wire, nb, remote, local, last_of_row, last_of_col, mirror_part, forward_part):
        self.place, self.wire, self.nb, self.hf = place, wire, nb, nb // 2
        self.cols, self.rows = remote[:2]
        self.ca, self.bp, self.bm, self.cp, self.cm, self.d, self.ep, self.em, self.gp, self.gm, self.v = remote[2:]
        self.mirror_sums, self.forward_sums, self.mo, self.s, self.sf = local
        self.last_of_row, self.last_of_col = last_of_row, last_of_col
        self.mirror_part, self.forward_part = mirror_part, forward_part
        self.near_slot, self.far_slot = wire.slot(), wire.slot()
        self.pieces = [place.z, place.pair, place.near_z, place.far_z]
        self.sums = [3 - place.z, (place.z + 2) % 4, place.pair, place.z]
        self.halves = [1 - place.h, place.h]
        self.made, self.cores = {}, []

    def run(self, codes):
        for code in codes:
            name, index = (code[:-1], int(code[-1])) if code[-1].isdigit() else (code, None)
            step = getattr(self, STEPS[name])
            step() if index is None else step(index)


    def cc(self, y, z, start=0, size=None):
        size = self.nb if size is None else size
        return self.cols.at[pl.ds(self.place.row_of(y=y, z=z) * self.nb + start, size)]

    def rr(self, x, h, start=0, size=None):
        size = self.nb if size is None else size
        return self.rows.at[pl.ds((x * 2 + h) * self.nb + start, size)]

    def same(self, key, ref, device, **options):
        self.made[key] = self.wire.send(ref, ref, device, **options)

    def arrived(self, *keys):
        for key in keys:
            self.made[key].wait_recv()

    def to_pair(self):
        self.same("pair", self.cc(self.place.y, self.place.z), self.place.at_z(self.place.pair))

    def to_middle(self):
        p = self.place
        self.same("near", self.cc(p.y, p.z), p.at_z(3 - p.z), recv=self.near_slot, when=p.inner)

    def pair_to_middle(self):
        p = self.place
        self.same("far", self.cc(p.y, p.pair), p.at_z(3 - p.z), recv=self.far_slot, when=p.inner)

    def near_to_pair(self):
        p = self.place
        self.same("near2", self.cc(p.y, p.near_z), p.at_z(p.pair), recv=self.near_slot, when=p.inner)

    def far_to_pair(self):
        p = self.place
        self.same("far2", self.cc(p.y, p.far_z), p.at_z(p.pair), recv=self.far_slot, when=p.inner)

    def wait_pair(self):
        self.arrived("pair")

    def wait_near(self):
        self.arrived("near")

    def wait_far(self):
        self.arrived("far")

    def along_y(self, k):
        p = self.place
        piece = self.cc(p.y, self.pieces[k])
        self.same(("up", k), piece, p.at_y(1))
        self.same(("down", k), piece, p.at_y(3))

    def core(self, y, k):
        piece = self.cc(y % 4, self.pieces[k])
        self.cores.append(self.wire.send(piece, piece, self.place.other_core()))

    def core_own(self, k):
        self.core(self.place.y, k)

    def core_next(self, k):
        self.core(self.place.y + 3, k)
        self.core(self.place.y + 1, k)

    def core_across(self, k):
        self.core(self.place.y + 2, k)

    def forward_y(self, k):
        p, hf = self.place, self.hf
        self.arrived(("up", k))
        self.same(("up half", k), self.cc((p.y + 3) % 4, self.pieces[k], 0, hf), p.at_y(1))
        self.arrived(("down", k))
        self.same(("down half", k), self.cc((p.y + 1) % 4, self.pieces[k], hf, hf), p.at_y(3))

    def wait_y(self, k):
        self.arrived(("up half", k), ("down half", k))

    def across(self):
        p = self.place
        self.same("z", self.rr(p.x, p.h), p.across_z())

    def wait_across(self):
        self.arrived("z")

    def along_x(self, i):
        p = self.place
        piece = self.rr(p.x, self.halves[1 - i])
        self.same(("right", i), piece, p.at_x(1))
        self.same(("left", i), piece, p.at_x(3))

    def forward_x(self, i):
        p, hf, h = self.place, self.hf, self.halves[1 - i]
        self.arrived(("right", i))
        self.same(("right half", i), self.rr((p.x + 3) % 4, h, 0, hf), p.at_x(1))
        self.arrived(("left", i))
        self.same(("left half", i), self.rr((p.x + 1) % 4, h, hf, hf), p.at_x(3))

    def wait_x(self):
        for i in range(2):
            self.arrived(("right half", i), ("left half", i))

    def wait_cores(self):
        for copy in self.cores:
            copy.wait_recv()


    def blocks(self, count, body):
        def step(b, carry):
            body(b)
            return carry

        lax.fori_loop(0, count, step, 0, unroll=4)

    def mirror_of(self, k, y, core, b):
        return self.mirror_sums[self.last_of_col(((y * 4 + self.sums[k]) * 2 + core) * self.nb + b)]

    def add(self, target, addend):
        def body(b):
            target[b] = target[b] + addend[b]

        self.blocks(self.hf, body)

    def send(self, key, src, dst, device):
        self.made[key] = self.wire.send(src, dst, device)

    def to_core(self, k):
        for y in range(4):

            def body(b):
                self.mo[k, y, b] = self.mirror_of(k, y, 1 - self.place.c, b).astype(BF16)

            self.blocks(self.nb, body)
        self.send(("core", k), self.mo.at[k], self.ca.at[k], self.place.other_core())

    def own(self, k, y):
        def body(b):
            mine = self.mirror_of(k, y, self.place.c, b)
            self.s[k, y, b] = (mine + self.ca[k, y, b].astype(F32)).astype(BF16)

        self.blocks(self.nb, body)

    def first_y(self, k):
        p, hf = self.place, self.hf
        across = (p.y + 2) % 4
        self.arrived(("core", k))
        self.own(k, across)
        self.send(("b up", k), self.s.at[k, across, pl.ds(0, hf)], self.bp.at[k], p.at_y(1))
        self.send(("b down", k), self.s.at[k, across, pl.ds(hf, hf)], self.bm.at[k], p.at_y(3))
        self.own(k, (p.y + 1) % 4)
        self.own(k, (p.y + 3) % 4)

    def second_y(self, k):
        p, hf = self.place, self.hf
        up, down = (p.y + 1) % 4, (p.y + 3) % 4
        self.arrived(("b up", k))
        self.add(self.s.at[k, up, pl.ds(0, hf)], self.bp.at[k])
        self.send(("c up", k), self.s.at[k, up], self.cp.at[k], p.at_y(1))
        self.arrived(("b down", k))
        self.add(self.s.at[k, down, pl.ds(hf, hf)], self.bm.at[k])
        self.send(("c down", k), self.s.at[k, down], self.cm.at[k], p.at_y(3))

    def home(self, k, b):
        total = self.mirror_of(k, self.place.y, self.place.c, b) + self.ca[k, self.place.y, b].astype(F32)
        return total + self.cp[k, b].astype(F32) + self.cm[k, b].astype(F32)

    def third_z(self, k):
        self.arrived(("c up", k), ("c down", k))
        target = self.s.at[k, self.place.y]

        def body(b):
            target[b] = self.home(k, b).astype(BF16)

        self.blocks(self.nb, body)
        self.send(("d", k), target, self.d.at[k], self.place.at_z(self.sums[k]))

    def first_x(self, k):
        p, hf = self.place, self.hf
        for x in range(4):

            def body(b):
                at = (x * 2 + self.halves[k]) * self.nb + b
                self.sf[k, x, b] = self.forward_sums[self.last_of_row(at)].astype(BF16)

            self.blocks(self.nb, body)
        across = (p.x + 2) % 4
        self.send(("e right", k), self.sf.at[k, across, pl.ds(0, hf)], self.ep.at[k], p.at_x(1))
        self.send(("e left", k), self.sf.at[k, across, pl.ds(hf, hf)], self.em.at[k], p.at_x(3))

    def second_x(self, k):
        p, hf = self.place, self.hf
        right, left = (p.x + 1) % 4, (p.x + 3) % 4
        self.arrived(("e right", k))
        self.add(self.sf.at[k, right, pl.ds(0, hf)], self.ep.at[k])
        self.send(("g right", k), self.sf.at[k, right], self.gp.at[k], p.at_x(1))
        self.arrived(("e left", k))
        self.add(self.sf.at[k, left, pl.ds(hf, hf)], self.em.at[k])
        self.send(("g left", k), self.sf.at[k, left], self.gm.at[k], p.at_x(3))

    def third_x(self):
        self.arrived(("g right", 0), ("g left", 0))
        target = self.sf.at[0, self.place.x]

        def body(b):
            total = target[b].astype(F32) + self.gp[0, b].astype(F32) + self.gm[0, b].astype(F32)
            target[b] = total.astype(BF16)

        self.blocks(self.nb, body)
        self.send("v", target, self.v, self.place.across_z())

    def wait_sums(self):
        self.arrived(("c up", 3), ("c down", 3), ("g right", 1), ("g left", 1))
        self.arrived(("d", 0), ("d", 1), ("d", 2), "v")

    def image(self, b):
        total = self.home(3, b)
        total = total + self.d[0, b].astype(F32) + self.d[1, b].astype(F32) + self.d[2, b].astype(F32)
        total = total + self.sf[1, self.place.x, b].astype(F32)
        total = total + self.gp[1, b].astype(F32) + self.gm[1, b].astype(F32)
        return total + self.v[b].astype(F32)


STEPS = dict(
    P="to_pair", N="to_middle", F="pair_to_middle", wp="wait_pair", wn="wait_near", wf="wait_far", y="along_y",
    c="core_own", C="core_next", D="core_across", Y="forward_y", L="wait_y", Z="across", wz="wait_across",
    x="along_x", X="forward_x", H="wait_x", K="wait_cores", M="mirror_part", S="forward_part", A="to_core",
    B="first_y", E="second_y", T="third_z", q="first_x", r="second_x", v="third_x", W="wait_sums",
)
STEPS["n>"], STEPS["f>"] = "near_to_pair", "far_to_pair"


REMOTE = 13


def filter_kernel(
    vectors, row_keys, col_keys, row_at, col_at, counts, center, radius, blocks_hbm, result,
    blocks, mirror_sums, forward_sums, mo, s, sf, current, found, tables, *rest,
):
    place = Place()
    barrier = pltpu.get_barrier_semaphore()
    partners = place.partners()
    for partner in partners:
        pl.semaphore_signal(barrier, inc=1, device_id=partner, device_id_type=MESH)
    products = [rest[:REMOTE], rest[REMOTE : 2 * REMOTE]]
    sems, block_sem, table_sem = rest[2 * REMOTE : -2], rest[-2], rest[-1]
    capacity, bs = blocks.shape[0], blocks.shape[1]
    nb = vectors.shape[1] // bs
    col_total, row_total = products[0][0].shape[0], products[0][1].shape[0]
    fetch = pltpu.make_async_copy(blocks_hbm, blocks, block_sem)
    fetch.start()
    k = vectors.shape[0]
    mirror_sums[capacity] = jnp.zeros((k, bs), F32)
    forward_sums[capacity] = jnp.zeros((k, bs), F32)
    before_in_row = lambda i: tables[0, i]
    before_in_col = lambda i: tables[0, capacity + i]
    last_of_row = lambda i: tables[0, 2 * capacity + i]
    last_of_col = lambda i: tables[0, 2 * capacity + row_total + i]
    span = capacity // PARTS

    def part_of(source, source_at, before, sums, contract):
        def part(index):
            first = index * span

            def body(i, carry):
                start = first + i * UNROLL
                terms = [
                    lax.dot_general(
                        source[source_at[start + u]],
                        blocks[start + u],
                        (((1,), (contract,)), ((), ())),
                        preferred_element_type=F32,
                    )
                    for u in range(UNROLL)
                ]
                for u in range(UNROLL):
                    sums[start + u] = terms[u] + sums[before(start + u)]
                return carry

            lax.fori_loop(0, span // UNROLL, body, 0)

        return part

    def put_own(cols_out, rows_out, b, value):
        narrow = value.astype(BF16)
        cols_out[place.row * nb + b] = narrow
        rows_out[place.col * nb + b] = narrow

    def make_tables():
        square = (capacity, capacity)
        down, along = lax.broadcasted_iota(jnp.int32, square, 0), lax.broadcasted_iota(jnp.int32, square, 1)
        count = counts[0]
        offset = 0

        def store(hits, size):
            nonlocal offset
            slots = lax.broadcasted_iota(jnp.int32, (capacity, size), 0)
            latest = jnp.max(jnp.where(hits, slots, -1), axis=0, keepdims=True)
            found[:, offset : offset + size] = jnp.where(latest < 0, capacity, latest)
            offset += size

        keys_down = []
        for keys in (row_keys, col_keys):
            spread = jnp.broadcast_to(keys[...], square)
            down_keys = jnp.sum(jnp.where(down == along, spread, 0), axis=1, keepdims=True)
            keys_down.append(down_keys)
            store((down_keys == spread) & (down < along) & (down < count), capacity)
        for down_keys, total in zip(keys_down, (row_total, col_total)):
            wanted = lax.broadcasted_iota(jnp.int32, (capacity, total), 1)
            live = lax.broadcasted_iota(jnp.int32, (capacity, total), 0) < count
            store((down_keys == wanted) & live, total)
        copy = pltpu.make_async_copy(found, tables, table_sem)
        copy.start()
        copy.wait()

    for b in range(nb):
        put_own(products[0][0], products[0][1], b, vectors[:, b * bs : (b + 1) * bs])
    pl.semaphore_wait(barrier, len(partners))
    for p in range(2):
        mirror_part = part_of(products[p][1], row_at, before_in_col, mirror_sums, 0)
        forward_part = part_of(products[p][0], col_at, before_in_row, forward_sums, 1)
        wire = Wire(sems[2 * p], sems[2 * p + 1])
        product = Product(
            place, wire, nb, products[p], (mirror_sums, forward_sums, mo, s, sf), last_of_row, last_of_col,
            mirror_part, forward_part,
        )
        tables_at = SCRIPT.index("|")
        product.run(SCRIPT[:tables_at])
        if p == 0:
            make_tables()
            fetch.wait()
        product.run(SCRIPT[tables_at + 1 :])
        for b in range(nb):
            part = slice(b * bs, (b + 1) * bs)
            if p == 0:
                value = (product.image(b) - center[0] * vectors[:, part]) / radius[0]
                current[:, part] = value
                put_own(products[1][0], products[1][1], b, value)
            else:
                value = 2.0 * (product.image(b) - center[0] * current[:, part]) / radius[0] - vectors[:, part]
                result[:, part] = value
        wire.drain()


def shards(vectors, block_values, block_rows, block_cols, block_counts, center, radius):
    k, own_rows = vectors.shape
    capacity, bs, _ = block_values.shape
    nb = own_rows // bs
    row_total = lax.axis_size("col") * nb
    col_total = lax.axis_size("row") * nb
    whole, half = (nb, k, bs), (nb // 2, k, bs)
    remote = [
        pltpu.VMEM((col_total, k, bs), BF16),
        pltpu.VMEM((row_total, k, bs), BF16),
        pltpu.VMEM((4, 4) + whole, BF16),
        pltpu.VMEM((4,) + half, BF16),
        pltpu.VMEM((4,) + half, BF16),
        pltpu.VMEM((4,) + whole, BF16),
        pltpu.VMEM((4,) + whole, BF16),
        pltpu.VMEM((3,) + whole, BF16),
        pltpu.VMEM((2,) + half, BF16),
        pltpu.VMEM((2,) + half, BF16),
        pltpu.VMEM((2,) + whole, BF16),
        pltpu.VMEM((2,) + whole, BF16),
        pltpu.VMEM(whole, BF16),
    ]
    return pl.pallas_call(
        filter_kernel,
        out_shape=jax.ShapeDtypeStruct((k, own_rows), F32),
        in_specs=[VMEM, VMEM, VMEM, SMEM, SMEM, SMEM, SMEM, SMEM, ANY],
        out_specs=VMEM,
        scratch_shapes=[
            pltpu.VMEM((capacity, bs, bs), BF16),
            pltpu.VMEM((capacity + 1, k, bs), F32),
            pltpu.VMEM((capacity + 1, k, bs), F32),
            pltpu.VMEM((4, 4) + whole, BF16),
            pltpu.VMEM((4, 4) + whole, BF16),
            pltpu.VMEM((2, 4) + whole, BF16),
            pltpu.VMEM((k, own_rows), F32),
            pltpu.VMEM((1, 2 * capacity + row_total + col_total), jnp.int32),
            pltpu.SMEM((1, 2 * capacity + row_total + col_total), jnp.int32),
        ]
        + remote * 2
        + [pltpu.SemaphoreType.DMA((COPIES,))] * 4
        + [pltpu.SemaphoreType.DMA] * 2,
        compiler_params=pltpu.CompilerParams(
            collective_id=0, has_side_effects=True, vmem_limit_bytes=56 * 2**20
        ),
        name="filter",
    )(
        vectors, block_rows.reshape(1, capacity), block_cols.reshape(1, capacity), block_rows, block_cols,
        block_counts, center, radius, block_values,
    )


def solution(mesh):
    return jax.shard_map(
        shards,
        mesh=mesh,
        in_specs=(
            P(None, ("row", "col")),
            P(("row", "col"), None, None),
            P(("row", "col")),
            P(("row", "col")),
            P(("row", "col")),
            P(),
            P(),
        ),
        out_specs=P(None, ("row", "col")),
        check_vma=False,
    )
```
